32 devices in a mesh: req: 32 (over z, y, x, core).
Axes of the slice: x: 2, y: 2, z: 4, core: 2. Of those that a mesh axis runs over, the one named last changes fastest.
Arguments:
- hidden_in: bfloat16 [16384, 2048], P('req'), may hold values from -6 to 6
- qkv: bfloat16 [16384, 6144], P('req'), may hold values from -400 to 400
- cache: bfloat16 [128, 128, 4096], P('req'), may hold values from -400 to 400
- lengths: int32 [128], P('req'), may hold values from 2 to 128, as said below
- prefill_flag: int32 [32], P('req'), may hold values 0 or 1
- cache_slot: int32 [128], P('req'), may hold values from 0 to 127, as said below
- slot_owner: int32 [128], P('req'), may hold values from 0 to 127, as said below
- out_weight: bfloat16 [2048, 2048], replicated, may hold values from -0.125 to 0.125
Outputs:
- layer_out: bfloat16 [16384, 2048], P('req')
The draws below stay inside these ranges and needn't reach their ends.
Inputs may be any that keep to these rules, and one draw needn't show every extreme that they name: Each slot stores exactly one request's cache; of each device's 4 requests, at least half have their cache in a slot of their own device, drawn which; slot_owner[cache_slot[r]] = r. `slot_owner`: the inverse of cache_slot. `lengths`: some slot holds exactly 128 valid positions.
All inputs are finite; a program needn't handle non-finite values. No bound on the sum of `prefill_flag` on one device may be relied on, other than what follows from the above.
Results may differ from the reference program's by a relative error of at most 0.0034.
Values may be sent and summed in bfloat16 or wider, within the bound.
A program may use at most 128 MiB of HBM per device.

```python
import math
import jax
import jax.numpy as jnp
from jax import lax

D = 2048
H = 16
HD = 128
TOK_DEV = 512
RD = 4
LMAX = 128
ROWS = 16384
SLOTS = 128
N_REQ = 32


def slot_tables(key):
    base = jax.random.fold_in(key, 101)
    shuffle = jax.random.permutation(jax.random.fold_in(base, 1), N_REQ).astype(jnp.int32)
    device_keys = jax.random.split(jax.random.fold_in(base, 2), N_REQ)
    inner = jax.vmap(lambda sub: jax.random.permutation(sub, RD))(device_keys).astype(jnp.int32)
    device_ids = jnp.arange(N_REQ, dtype=jnp.int32)[:, None]
    positions = jnp.arange(RD, dtype=jnp.int32)[None, :]
    holders = jnp.where(positions < RD // 2, device_ids, shuffle[:, None])
    slot_ids = (holders * RD + positions).reshape(-1)
    request_ids = (device_ids * RD + inner).reshape(-1)
    cache_slot = jnp.zeros((SLOTS,), jnp.int32).at[request_ids].set(slot_ids)
    slot_owner = jnp.zeros((SLOTS,), jnp.int32).at[slot_ids].set(request_ids)
    return (cache_slot, slot_owner)


def first_keys(key):
    return jnp.clip(jax.random.normal(jax.random.fold_in(key, 102), (SLOTS, D), jnp.float32), -6.0, 6.0)


def base_values(key, shape):
    return jnp.clip(jax.random.normal(key, shape, jnp.float32), -6.0, 6.0)


def draw_cache_slot(key, part):
    return slot_tables(key)[0]


def draw_slot_owner(key, part):
    return slot_tables(key)[1]


def draw_lengths(key, part):
    drawn = jax.random.randint(jax.random.fold_in(key, 401), (SLOTS,), 2, LMAX + 1).astype(jnp.int32)
    chosen = jax.random.randint(jax.random.fold_in(key, 402), (), 0, SLOTS)
    return drawn.at[chosen].set(LMAX)


def draw_cache(key, part):
    values = base_values(jax.random.fold_in(key, 201), (SLOTS, LMAX, 2 * D))
    leading = first_keys(key)
    values = values.at[:, 0, :D].set(leading)
    return values.astype(jnp.bfloat16)


def draw_qkv(key, part):
    values = base_values(jax.random.fold_in(key, 301), (ROWS, 3 * D))
    return values.astype(jnp.bfloat16)


def set_ends(values, stream_key, least, largest):
    shape = values.shape
    spot = [jax.random.randint(jax.random.fold_in(stream_key, axis), (), 0, shape[axis]) for axis in range(len(shape))]
    values = values.at[tuple(spot)].set(least)
    longest = shape.index(max(shape))
    spot[longest] = (spot[longest] + 1) % shape[longest]
    return values.at[tuple(spot)].set(largest)


def block_levels(stream_key, extent, cuts, least, high):
    gain = 1.0
    for axis_at, blocks in cuts:
        steps = jax.random.uniform(jax.random.fold_in(jax.random.fold_in(stream_key, 6), axis_at), (blocks,), jnp.float32, least / len(cuts), high / len(cuts))
        gain = gain * jnp.repeat(jnp.exp(steps), extent[axis_at] // blocks).reshape((-1,) + (1,) * (len(extent) - 1 - axis_at))
    return gain


def scatter_about(key, dims, deviation, reach, cuts=(), kind=jnp.bfloat16):
    array = deviation * jax.random.normal(key, dims, jnp.float32)
    if cuts:
        array = array * block_levels(key, dims, cuts, -0.22, 0.18)
    return jnp.clip(array, -reach, reach).astype(kind)


def setup_inputs(seed: int = 0) -> dict:
    splits = jax.random.split(jax.random.key(seed), 9)
    return {
        "hidden_in": scatter_about(splits[0], (ROWS, D), 1.0, 6.0, ((0, 32),)),
        "qkv": draw_qkv(jax.random.fold_in(splits[8], 71), 0),
        "cache": draw_cache(jax.random.fold_in(splits[8], 71), 0),
        "lengths": draw_lengths(jax.random.fold_in(splits[8], 71), 0),
        "prefill_flag": set_ends((jax.random.randint(splits[4], (N_REQ,), 0, 2) < 1).astype(jnp.int32), jax.random.fold_in(splits[4], 1), 0, 1),
        "cache_slot": draw_cache_slot(jax.random.fold_in(splits[8], 71), 0),
        "slot_owner": draw_slot_owner(jax.random.fold_in(splits[8], 71), 0),
        "out_weight": scatter_about(splits[7], (D, D), D ** -0.5, 0.125),
    }


def prefill_block(block):
    score_scale = 1.0 / math.sqrt(HD)
    queries = block[:, :D].reshape(TOK_DEV, H, HD).astype(jnp.float32)
    keys_new = block[:, D:2 * D].reshape(TOK_DEV, H, HD).astype(jnp.float32)
    values_new = block[:, 2 * D:].reshape(TOK_DEV, H, HD).astype(jnp.float32)
    scores = jnp.einsum('qhd,khd->hqk', queries, keys_new) * score_scale
    causal = jnp.arange(TOK_DEV)[:, None] >= jnp.arange(TOK_DEV)[None, :]
    scores = jnp.where(causal[None], scores, -jnp.inf)
    top_score = lax.optimization_barrier(jnp.max(scores, axis=-1, keepdims=True))
    expon = jnp.exp(scores - top_score)
    totals = lax.optimization_barrier(jnp.sum(expon, axis=-1))
    rounded = lax.optimization_barrier(expon.astype(jnp.bfloat16)).astype(jnp.float32)
    summed = jnp.einsum('hqk,khd->qhd', rounded, values_new)
    result = summed / jnp.transpose(totals)[:, :, None]
    return result.reshape(TOK_DEV, D).astype(jnp.bfloat16)

def slot_partial(pieces):
    queries, stored, slot_lengths = pieces
    score_scale = 1.0 / math.sqrt(HD)
    query_heads = queries.reshape(RD, H, HD).astype(jnp.float32)
    cache_keys = stored[:, :, :D].reshape(RD, LMAX, H, HD).astype(jnp.float32)
    cache_values = stored[:, :, D:].reshape(RD, LMAX, H, HD).astype(jnp.float32)
    valid = jnp.arange(LMAX, dtype=jnp.int32)[None, None, :] < slot_lengths[:, None, None]
    scores = jnp.einsum('rhd,rlhd->rhl', query_heads, cache_keys) * score_scale
    scores = jnp.where(valid, scores, -jnp.inf)
    cache_max = lax.optimization_barrier(jnp.max(scores, axis=-1))
    expon = jnp.exp(scores - cache_max[..., None])
    cache_total = lax.optimization_barrier(jnp.sum(expon, axis=-1))
    rounded = lax.optimization_barrier(expon.astype(jnp.bfloat16)).astype(jnp.float32)
    cache_out = jnp.einsum('rhl,rlhd->rhd', rounded, cache_values)
    return (cache_out, cache_max, cache_total)

def reference(hidden_in, qkv, cache, lengths, prefill_flag, cache_slot, slot_owner, out_weight):
    blocks = qkv.reshape(N_REQ, TOK_DEV, 3 * D)
    prefill_att = lax.map(prefill_block, blocks)
    request_rows = blocks[:, :RD, :].reshape(SLOTS, 3 * D)
    slot_queries = request_rows[slot_owner][:, :D]
    part_out, part_max, part_total = lax.map(slot_partial, (slot_queries.reshape(N_REQ, RD, D), cache.reshape(N_REQ, RD, LMAX, 2 * D), lengths.reshape(N_REQ, RD)))
    part_out = part_out.reshape(SLOTS, H, HD)[cache_slot]
    part_max = part_max.reshape(SLOTS, H)[cache_slot]
    part_total = part_total.reshape(SLOTS, H)[cache_slot]
    score_scale = 1.0 / math.sqrt(HD)
    queries = request_rows[:, :D].reshape(SLOTS, H, HD).astype(jnp.float32)
    keys_new = request_rows[:, D:2 * D].reshape(SLOTS, H, HD).astype(jnp.float32)
    values_new = request_rows[:, 2 * D:].reshape(SLOTS, H, HD).astype(jnp.float32)
    own_score = lax.optimization_barrier(jnp.sum(queries * keys_new, axis=-1)) * score_scale
    joint_max = jnp.maximum(part_max, own_score)
    cache_factor = jnp.exp(part_max - joint_max)
    own_factor = jnp.exp(own_score - joint_max)
    numer = part_out * cache_factor[..., None] + own_factor[..., None] * values_new
    denom = part_total * cache_factor + own_factor
    decode_att = (numer / denom[..., None]).reshape(N_REQ, RD, D).astype(jnp.bfloat16)
    padding = jnp.zeros((N_REQ, TOK_DEV - RD, D), jnp.bfloat16)
    decode_rows = jnp.concatenate([decode_att, padding], axis=1)
    attended = jnp.where(prefill_flag[:, None, None] == 1, prefill_att, decode_rows)
    projected = jnp.dot(attended.reshape(ROWS, D), out_weight, preferred_element_type=jnp.float32).astype(jnp.bfloat16)
    summed = hidden_in.astype(jnp.float32) + projected.astype(jnp.float32)
    return summed.astype(jnp.bfloat16)
```

```python
import functools
import math

import jax
import jax.numpy as jnp
from jax import lax
from jax.experimental import pallas as pl
from jax.experimental.pallas import tpu as pltpu
from jax.sharding import PartitionSpec as P

D = 2048
H = 16
HD = 128
TOK_DEV = 512
RD = 4
LMAX = 128
HALF = TOK_DEV // 2
CUTS = ((0, 5), (5, 10), (10, 13), (13, 16))
UP = 256
COLS = 512
NT = 512
SPLIT = 1024
EXT = D + HD
MARK = 96
SCALE = 1.0 / math.sqrt(HD)
SCALE2 = SCALE * math.log2(math.e)
F32 = jnp.float32
BF16 = jnp.bfloat16
MESH = pl.DeviceIdType.MESH
NEG = float(jnp.finfo(jnp.float32).min)


def score(x, y):
    return lax.dot_general(x, y, (((1,), (1,)), ((), ())), preferred_element_type=F32)


def attend_head(h, qkv, att):
    col = h * HD
    q = qkv[0, :, pl.ds(col, HD)]
    keys = qkv[1, :, pl.ds(col, HD)]
    ones = jnp.ones((TOK_DEV, HD), BF16)
    values = jnp.concatenate([qkv[2, :, pl.ds(col, HD)], ones], axis=1)
    row = lax.broadcasted_iota(jnp.int32, (HALF, HALF), 0)
    lane = lax.broadcasted_iota(jnp.int32, (HALF, HALF), 1)
    causal = lane <= row
    s_first = score(q, keys[:HALF])
    s_last = jnp.where(causal, score(q[HALF:], keys[HALF:]), NEG)
    s_upper = jnp.where(causal, s_first[:HALF], NEG)
    s_lower = s_first[HALF:]
    top_upper = jnp.max(s_upper, axis=1, keepdims=True)
    top_lower = jnp.max(jnp.maximum(s_lower, s_last), axis=1, keepdims=True)
    p_upper = jnp.exp2((s_upper - top_upper) * SCALE2).astype(BF16)
    p_lower = jnp.exp2((s_lower - top_lower) * SCALE2).astype(BF16)
    p_last = jnp.exp2((s_last - top_lower) * SCALE2).astype(BF16)
    lower = jnp.dot(
        jnp.concatenate([p_lower, p_last], axis=1), values, preferred_element_type=F32
    )
    upper = jnp.dot(p_upper, values[:HALF], preferred_element_type=F32)
    att[pl.ds(0, HALF), pl.ds(col, HD)] = (upper[:, :HD] / upper[:, HD:]).astype(BF16)
    att[pl.ds(HALF, HALF), pl.ds(col, HD)] = (lower[:, :HD] / lower[:, HD:]).astype(BF16)


def head_mask():
    row = lax.broadcasted_iota(jnp.int32, (H, D), 0)
    lane = lax.broadcasted_iota(jnp.int32, (H, D), 1)
    return (lane // HD) == row


def pick_row(block, j):
    row = lax.broadcasted_iota(jnp.int32, block.shape, 0)
    return jnp.sum(jnp.where(row == j, block.astype(F32), 0.0), axis=0, keepdims=True)


def pick_marked(block, place):
    block = block.astype(F32)
    lane = lax.broadcasted_iota(jnp.int32, (2, HD), 1)
    mark = jnp.sum(jnp.where(lane == MARK, block[:, D:], 0.0), axis=1, keepdims=True)
    wanted = mark == place.astype(F32)
    return jnp.sum(jnp.where(wanted, block, 0.0), axis=0, keepdims=True)


def split3(x):
    pieces = []
    for _ in range(3):
        piece = x.astype(BF16).astype(F32)
        pieces.append(piece)
        x = x - piece
    return pieces


def first_two(far):
    one = jnp.int32(-1)
    two = jnp.int32(-1)
    for j in reversed(range(RD)):
        two = jnp.where(far[j], one, two)
        one = jnp.where(far[j], jnp.int32(j), one)
    return one, two


def message(rows, places):
    lane = lax.broadcasted_iota(jnp.int32, (1, EXT), 1)
    row = lax.broadcasted_iota(jnp.int32, (2, EXT), 0)
    marked = [
        jnp.where(lane == D + MARK, place.astype(F32), x) for x, place in zip(rows, places)
    ]
    return jnp.where(row == 0, marked[0], marked[1]).astype(BF16)


def partial(q, slot, cache, lengths, own):
    valid = lax.broadcasted_iota(jnp.int32, (H, LMAX), 1) < lengths[slot]
    q_heads = jnp.where(own, q, 0.0).astype(BF16)
    scores = jnp.where(valid, score(q_heads, cache[slot, :, pl.ds(0, D)]), NEG)
    top = jnp.max(scores, axis=1, keepdims=True)
    p = jnp.where(valid, jnp.exp2((scores - top) * SCALE2), 0.0)
    total = jnp.sum(p, axis=1, keepdims=True)
    o = jnp.dot(p.astype(BF16), cache[slot, :, pl.ds(D, D)], preferred_element_type=F32)
    o = jnp.sum(jnp.where(own, o / total, 0.0), axis=0, keepdims=True)
    row = lax.broadcasted_iota(jnp.int32, (H, HD), 0)
    lane = lax.broadcasted_iota(jnp.int32, (H, HD), 1)
    stats = jnp.zeros((H, HD), F32)
    for k, piece in enumerate(split3(top * SCALE) + split3(total)):
        stats = jnp.where(lane == row + k * H, piece, stats)
    return jnp.concatenate([o, jnp.sum(stats, axis=0, keepdims=True)], axis=1)


def kernel(
    nc,
    lengths_hbm,
    flag,
    where_hbm,
    owner_hbm,
    hidden_hbm,
    qkv_hbm,
    cache_hbm,
    weight_hbm,
    flag_any,
    att_any,
    low_any,
    weight_any,
    lengths,
    where,
    owners,
    first,
    hidden,
    qkv,
    cache,
    weight,
    att,
    low,
    flags,
    local_part,
    qg,
    cg,
    in_sem,
    out_sem,
    send_q,
    recv_q,
    send_c,
    recv_c,
    pair_q,
    pair_c,
):
    me = lax.axis_index("req")
    chip = me // 2
    core = me % 2
    partner = chip * 2 + 1 - core

    def peer(t):
        return lax.rem(chip + t, nc) * 2 + core

    small = [
        pltpu.make_async_copy(src, dst, in_sem.at[i])
        for i, (src, dst) in enumerate(
            [
                (where_hbm, where),
                (owner_hbm, owners),
                (lengths_hbm, lengths),
                (qkv_hbm.at[pl.ds(0, 16), :], first),
            ]
        )
    ]
    load_cache = pltpu.make_async_copy(cache_hbm, cache, in_sem.at[5])
    load_weight = pltpu.make_async_copy(weight_hbm, weight, in_sem.at[6])
    load_hidden = pltpu.make_async_copy(hidden_hbm.at[pl.ds(UP, TOK_DEV - UP), :], hidden, in_sem.at[7])
    keep_weight = pltpu.make_async_copy(weight_hbm, weight_any, out_sem.at[0])
    loads = []
    for start, stop in CUTS:
        for part in range(3):
            loads.append(
                pltpu.make_async_copy(
                    qkv_hbm.at[:, pl.ds(part * D + start * HD, (stop - start) * HD)],
                    qkv.at[part, :, pl.ds(start * HD, (stop - start) * HD)],
                    in_sem.at[8 + len(loads)],
                )
            )
    for load in small:
        load.start()

    barrier = pltpu.get_barrier_semaphore()

    @pl.loop(1, nc)
    def _(t):
        pl.semaphore_signal(barrier, inc=1, device_id=(peer(t),), device_id_type=MESH)

    pl.semaphore_signal(barrier, inc=1, device_id=(partner,), device_id_type=MESH)

    for load in loads[:6]:
        load.start()
    load_cache.start()
    for load in loads[6:]:
        load.start()
    load_weight.start()
    load_hidden.start()
    keep_weight.start()

    def chip_copy(buf, send, recv, t):
        return pltpu.make_async_remote_copy(
            src_ref=buf.at[core, chip],
            dst_ref=buf.at[core, chip],
            send_sem=send.at[t - 1],
            recv_sem=recv.at[t - 1],
            device_id=(peer(t),),
            device_id_type=MESH,
        )

    def pair_copy(buf, pair):
        return pltpu.make_async_remote_copy(
            src_ref=buf.at[core],
            dst_ref=buf.at[core],
            send_sem=pair.at[0],
            recv_sem=pair.at[1],
            device_id=(partner,),
            device_id_type=MESH,
        )

    def start_chips(buf, send, recv):
        @pl.loop(1, nc)
        def _(t):
            chip_copy(buf, send, recv, t).start()

    def wait_chips(buf, send, recv):
        @pl.loop(1, nc)
        def _(t):
            chip_copy(buf, send, recv, t).wait()

    def segment(g):
        for load in loads[3 * g : 3 * g + 3]:
            load.wait()
        start, stop = CUTS[g]

        for h in range(start, stop):
            attend_head(h, qkv, att)

    for load in small:
        load.wait()
    own = head_mask()
    mine = first[...].astype(F32)[:8]
    places = first_two([where[j] // RD != me for j in range(RD)])
    no_stats = jnp.zeros((1, HD), F32)
    qg[core, chip] = message(
        [jnp.concatenate([pick_row(mine[:, :D], j), no_stats], axis=1) for j in places], places
    )
    pl.semaphore_wait(barrier, nc)
    start_chips(qg, send_q, recv_q)
    segment(0)
    segment(1)
    wait_chips(qg, send_q, recv_q)
    pair_copy(qg, pair_q).start()
    segment(2)
    load_cache.wait()
    pair_copy(qg, pair_q).wait()

    places = first_two([owners[s] // RD != me for s in range(RD)])
    rows = []
    for place in places:
        slot = jnp.maximum(place, 0)
        owner = owners[slot]
        device = owner // RD
        q = pick_marked(qg[device % 2, device // 2], owner % RD)
        rows.append(partial(q[:, :D], slot, cache, lengths, own))
    cg[core, chip] = message(rows, places)

    start_chips(cg, send_c, recv_c)
    row8 = lax.broadcasted_iota(jnp.int32, (8, EXT), 0)
    held = jnp.zeros((8, EXT), F32)
    for j in range(RD):
        part = partial(mine[j : j + 1, :D], where[j] % RD, cache, lengths, own)
        held = jnp.where(row8 == j, part, held)
    local_part[...] = held
    segment(3)
    load_weight.wait()
    load_hidden.wait()
    is_prefill = flag[0] == 1

    flags[...] = jnp.full((8, HD), flag[0], jnp.int32).astype(F32)
    keep_flag = pltpu.make_async_copy(flags, flag_any, out_sem.at[1])
    keep_flag.start()
    keep_att = pltpu.make_async_copy(
        att.at[pl.ds(H, UP - H), :], att_any.at[pl.ds(H, UP - H), :], out_sem.at[2]
    )
    keep_att.start()

    def project(first_col, last_col):
        @pl.loop(first_col // NT, last_col // NT)
        def _(n):
            cols = pl.ds(pl.multiple_of(n * NT, NT), NT)
            rows = pl.ds(UP, TOK_DEV - UP)
            acc = jnp.dot(att[rows, :], weight[:, cols], preferred_element_type=F32)
            acc = jnp.where(is_prefill, acc, 0.0).astype(BF16).astype(F32)
            low[:, cols] = (hidden[:, cols].astype(F32) + acc).astype(BF16)

    own_scores = []
    for j in range(RD):
        product = mine[j : j + 1, :D] * mine[j : j + 1, D : 2 * D]
        own_scores.append(
            jnp.sum(jnp.where(own, product, 0.0), axis=1, keepdims=True) * SCALE
        )

    project(0, SPLIT)
    wait_chips(cg, send_c, recv_c)
    pair_copy(cg, pair_c).start()
    project(SPLIT, D)
    keep_low = pltpu.make_async_copy(low, low_any, out_sem.at[3])
    keep_low.start()
    pair_copy(cg, pair_c).wait()

    row16 = lax.broadcasted_iota(jnp.int32, (H, D), 0)
    row_h = lax.broadcasted_iota(jnp.int32, (H, HD), 0)
    lane_h = lax.broadcasted_iota(jnp.int32, (H, HD), 1)
    diagonal = lane_h % H == row_h
    is_max = jnp.logical_and(diagonal, lane_h < 3 * H)
    is_total = jnp.logical_and(
        diagonal, jnp.logical_and(lane_h >= 3 * H, lane_h < 6 * H)
    )
    decoded = jnp.zeros((H, D), F32)
    for j in range(RD):
        slot = where[j]
        device = slot // RD
        far = pick_marked(cg[device % 2, device // 2], slot % RD)
        part = jnp.where(device == me, local_part[j : j + 1, :], far)
        co = part[:, :D]
        cm = jnp.sum(jnp.where(is_max, part[:, D:], 0.0), axis=1, keepdims=True)
        cl = jnp.sum(jnp.where(is_total, part[:, D:], 0.0), axis=1, keepdims=True)
        row = mine[j : j + 1]
        ns = own_scores[j]
        joint = jnp.maximum(cm, ns)
        wc = cl * jnp.exp(cm - joint)
        wo = jnp.exp(ns - joint)
        mixed = co * (wc / (wc + wo)) + row[:, 2 * D :] * (wo / (wc + wo))
        decoded = jnp.where(
            row16 == j, jnp.sum(jnp.where(own, mixed, 0.0), axis=0, keepdims=True), decoded
        )
    kept = jnp.where(is_prefill, att[pl.ds(0, H), :].astype(F32), decoded)
    att[pl.ds(0, H), :] = kept.astype(BF16)
    keep_top = pltpu.make_async_copy(
        att.at[pl.ds(0, H), :], att_any.at[pl.ds(0, H), :], out_sem.at[4]
    )
    keep_top.start()
    keep_weight.wait()
    keep_flag.wait()
    keep_att.wait()
    keep_low.wait()
    keep_top.wait()


def finish(flag, att, low, weight, hidden, out_hbm, out, sem):
    is_prefill = jnp.max(flag[...]) > 0.5
    store_low = pltpu.make_async_copy(low, out_hbm.at[pl.ds(UP, TOK_DEV - UP), :], sem.at[0])
    store_low.start()

    def project(rows, n):
        cols = pl.ds(n * COLS, COLS)
        acc = jnp.dot(att[pl.ds(0, rows), :], weight[:, cols], preferred_element_type=F32)
        acc = acc.astype(BF16).astype(F32)
        out[pl.ds(0, rows), cols] = (hidden[pl.ds(0, rows), cols].astype(F32) + acc).astype(BF16)
        store = pltpu.make_async_copy(
            out.at[pl.ds(0, rows), cols], out_hbm.at[pl.ds(0, rows), cols], sem.at[2 + n]
        )
        store.start()
        return store

    @pl.when(is_prefill)
    def _():
        for store in [project(UP, n) for n in range(D // COLS)]:
            store.wait()

    @pl.when(jnp.logical_not(is_prefill))
    def _():
        rest = pl.ds(H, UP - H)
        store_rest = pltpu.make_async_copy(hidden.at[rest, :], out_hbm.at[rest, :], sem.at[1])
        store_rest.start()
        for store in [project(H, n) for n in range(D // COLS)]:
            store.wait()
        store_rest.wait()

    store_low.wait()


def local(hidden_in, qkv, cache, lengths, prefill_flag, cache_slot, slot_owner, out_weight, n):
    nc = n // 2
    hbm = pl.BlockSpec(memory_space=pltpu.HBM)
    dma = pltpu.SemaphoreType.DMA
    vmem = pl.BlockSpec(memory_space=pltpu.VMEM)
    keep = [
        jax.ShapeDtypeStruct((8, HD), F32),
        jax.ShapeDtypeStruct((UP, D), BF16),
        jax.ShapeDtypeStruct((TOK_DEV - UP, D), BF16),
        jax.ShapeDtypeStruct((D, D), BF16),
    ]
    args = [
        x if x.shape == (1,) else pltpu.with_memory_space_constraint(x, pltpu.HBM)
        for x in (lengths, prefill_flag, cache_slot, slot_owner, hidden_in, qkv, cache, out_weight)
    ]
    kept = pl.pallas_call(
        functools.partial(kernel, nc),
        out_shape=keep,
        in_specs=[hbm, pl.BlockSpec(memory_space=pltpu.SMEM)] + [hbm] * 6,
        out_specs=[pl.BlockSpec(memory_space=pl.ANY)] * 4,
        scratch_shapes=[
            pltpu.SMEM((RD,), jnp.int32),
            pltpu.SMEM((RD,), jnp.int32),
            pltpu.SMEM((RD,), jnp.int32),
            pltpu.VMEM((16, 3 * D), BF16),
            pltpu.VMEM((TOK_DEV - UP, D), BF16),
            pltpu.VMEM((3, TOK_DEV, D), BF16),
            pltpu.VMEM((RD, LMAX, 2 * D), BF16),
            pltpu.VMEM((D, D), BF16),
            pltpu.VMEM((TOK_DEV, D), BF16),
            pltpu.VMEM((TOK_DEV - UP, D), BF16),
            pltpu.VMEM((8, HD), F32),
            pltpu.VMEM((8, EXT), F32),
            pltpu.VMEM((2, nc, 2, EXT), BF16),
            pltpu.VMEM((2, nc, 2, EXT), BF16),
            dma((8 + 3 * len(CUTS),)),
            dma((5,)),
            dma((nc - 1,)),
            dma((nc - 1,)),
            dma((nc - 1,)),
            dma((nc - 1,)),
            dma((2,)),
            dma((2,)),
        ],
        compiler_params=pltpu.CompilerParams(
            collective_id=0, has_side_effects=True, vmem_limit_bytes=34 * 1024 * 1024
        ),
    )(*args)
    return pl.pallas_call(
        finish,
        out_shape=jax.ShapeDtypeStruct((TOK_DEV, D), BF16),
        in_specs=[vmem] * 5,
        out_specs=hbm,
        scratch_shapes=[pltpu.VMEM((UP, D), BF16), dma((2 + D // COLS,))],
        compiler_params=pltpu.CompilerParams(vmem_limit_bytes=34 * 1024 * 1024),
    )(*kept, hidden_in)


def solution(mesh):
    placed = (
        P("req", None),
        P("req", None),
        P("req", None, None),
        P("req"),
        P("req"),
        P("req"),
        P("req"),
        P(),
    )
    return jax.shard_map(
        functools.partial(local, n=mesh.shape["req"]),
        mesh=mesh,
        in_specs=placed,
        out_specs=P("req", None),
        check_vma=False,
    )
```

```python
import functools
import math

import jax
import jax.numpy as jnp
from jax import lax
from jax.experimental import pallas as pl
from jax.experimental.pallas import tpu as pltpu
from jax.sharding import PartitionSpec as P

D = 2048
H = 16
HD = 128
TOK_DEV = 512
RD = 4
LMAX = 128
HALF = TOK_DEV // 2
CUTS = ((0, 3), (3, 9), (9, 16))
UP = 128
COLS = 512
NT = 512
SPLIT = 1536
EXT = D + HD
MARK = 96
SCALE = 1.0 / math.sqrt(HD)
SCALE2 = SCALE * math.log2(math.e)
F32 = jnp.float32
BF16 = jnp.bfloat16
MESH = pl.DeviceIdType.MESH
NEG = float(jnp.finfo(jnp.float32).min)


def score(x, y):
    return lax.dot_general(x, y, (((1,), (1,)), ((), ())), preferred_element_type=F32)


def head_scores(h, qkv):
    q = qkv[0, :, pl.ds(h * HD, HD)]
    keys = qkv[1, :, pl.ds(h * HD, HD)]
    return score(q, keys[:HALF]), score(q[HALF:], keys[HALF:])


def head_weights(scores):
    s_first, s_last = scores
    row = lax.broadcasted_iota(jnp.int32, (HALF, HALF), 0)
    lane = lax.broadcasted_iota(jnp.int32, (HALF, HALF), 1)
    causal = lane <= row
    s_last = jnp.where(causal, s_last, NEG)
    s_upper = jnp.where(causal, s_first[:HALF], NEG)
    s_lower = s_first[HALF:]
    top_upper = jnp.max(s_upper, axis=1, keepdims=True)
    top_lower = jnp.max(jnp.maximum(s_lower, s_last), axis=1, keepdims=True)
    return [
        jnp.exp2((s - top) * SCALE2).astype(BF16)
        for s, top in ((s_upper, top_upper), (s_lower, top_lower), (s_last, top_lower))
    ]


def head_values(h, weights, qkv, att):
    p_upper, p_lower, p_last = weights
    ones = jnp.ones((TOK_DEV, HD), BF16)
    values = jnp.concatenate([qkv[2, :, pl.ds(h * HD, HD)], ones], axis=1)
    lower = jnp.dot(
        jnp.concatenate([p_lower, p_last], axis=1), values, preferred_element_type=F32
    )
    upper = jnp.dot(p_upper, values[:HALF], preferred_element_type=F32)
    cols = pl.ds(h * HD, HD)
    att[pl.ds(0, HALF), cols] = (upper[:, :HD] / upper[:, HD:]).astype(BF16)
    att[pl.ds(HALF, HALF), cols] = (lower[:, :HD] / lower[:, HD:]).astype(BF16)


def attend(start, stop, qkv, att):
    scores = head_scores(start, qkv)
    for h in range(start, stop):
        later = head_scores(h + 1, qkv) if h + 1 < stop else None
        head_values(h, head_weights(scores), qkv, att)
        scores = later


def head_mask():
    row = lax.broadcasted_iota(jnp.int32, (H, D), 0)
    lane = lax.broadcasted_iota(jnp.int32, (H, D), 1)
    return (lane // HD) == row


def pick_row(block, j):
    row = lax.broadcasted_iota(jnp.int32, block.shape, 0)
    return jnp.sum(jnp.where(row == j, block.astype(F32), 0.0), axis=0, keepdims=True)


def pick_marked(block, place):
    block = block.astype(F32)
    lane = lax.broadcasted_iota(jnp.int32, (2, HD), 1)
    mark = jnp.sum(jnp.where(lane == MARK, block[:, D:], 0.0), axis=1, keepdims=True)
    wanted = mark == place.astype(F32)
    return jnp.sum(jnp.where(wanted, block, 0.0), axis=0, keepdims=True)


def split3(x):
    pieces = []
    for _ in range(3):
        piece = x.astype(BF16).astype(F32)
        pieces.append(piece)
        x = x - piece
    return pieces


def first_two(far):
    one = jnp.int32(-1)
    two = jnp.int32(-1)
    for j in reversed(range(RD)):
        two = jnp.where(far[j], one, two)
        one = jnp.where(far[j], jnp.int32(j), one)
    return one, two


def two_rows(rows):
    row = lax.broadcasted_iota(jnp.int32, (2, EXT), 0)
    return jnp.where(row == 0, rows[0], rows[1]).astype(BF16)


def message(rows, places):
    lane = lax.broadcasted_iota(jnp.int32, (1, EXT), 1)
    marked = [
        jnp.where(lane == D + MARK, place.astype(F32), x) for x, place in zip(rows, places)
    ]
    return two_rows(marked)


def partials(queries, slots, cache, lengths, own):
    row = lax.broadcasted_iota(jnp.int32, (H, HD), 0)
    lane = lax.broadcasted_iota(jnp.int32, (H, HD), 1)
    scores = []
    for q, slot in zip(queries, slots):
        q_heads = jnp.where(own, q, 0.0).astype(BF16)
        scores.append(score(q_heads, cache[slot, :, pl.ds(0, D)]))
    weights = []
    for s, slot in zip(scores, slots):
        valid = lax.broadcasted_iota(jnp.int32, (H, LMAX), 1) < lengths[slot]
        s = jnp.where(valid, s, NEG)
        top = jnp.max(s, axis=1, keepdims=True)
        p = jnp.where(valid, jnp.exp2((s - top) * SCALE2), 0.0)
        weights.append((p.astype(BF16), top, jnp.sum(p, axis=1, keepdims=True)))
    sums = []
    for (p, _, _), slot in zip(weights, slots):
        o = jnp.dot(p, cache[slot, :, pl.ds(D, D)], preferred_element_type=F32)
        sums.append(jnp.sum(jnp.where(own, o, 0.0), axis=0, keepdims=True))
    parts = []
    for o, (_, top, total) in zip(sums, weights):
        stats = jnp.zeros((H, HD), F32)
        for k, piece in enumerate(split3(top * SCALE) + split3(total)):
            stats = jnp.where(lane == row + k * H, piece, stats)
        parts.append(jnp.concatenate([o, jnp.sum(stats, axis=0, keepdims=True)], axis=1))
    return parts


def kernel(
    nc,
    lengths_hbm,
    flag,
    where_hbm,
    owner_hbm,
    hidden_hbm,
    qkv_hbm,
    cache_hbm,
    weight_hbm,
    flag_any,
    att_any,
    low_any,
    weight_any,
    lengths,
    where,
    owners,
    pair_where,
    pair_owners,
    first,
    hidden,
    qkv,
    cache,
    weight,
    att,
    low,
    flags,
    local_part,
    qg,
    cg,
    relay_q,
    relay_c,
    in_sem,
    out_sem,
    chip_sem,
    pair_sem,
):
    me = lax.axis_index("req")
    chip = me // 2
    core = me % 2
    partner = chip * 2 + 1 - core

    def peer(t):
        return lax.rem(chip + t, nc) * 2 + core

    small = [
        pltpu.make_async_copy(src, dst, in_sem.at[i])
        for i, (src, dst) in enumerate(
            [
                (where_hbm, where),
                (owner_hbm, owners),
                (lengths_hbm, lengths),
                (qkv_hbm.at[pl.ds(0, 16), :], first),
            ]
        )
    ]
    load_cache = pltpu.make_async_copy(cache_hbm, cache, in_sem.at[5])
    load_weight = pltpu.make_async_copy(weight_hbm, weight, in_sem.at[6])
    load_hidden = pltpu.make_async_copy(hidden_hbm.at[pl.ds(UP, TOK_DEV - UP), :], hidden, in_sem.at[7])
    keep_weight = pltpu.make_async_copy(weight_hbm, weight_any, out_sem.at[0])
    loads = []
    for start, stop in CUTS:
        for part in range(3):
            loads.append(
                pltpu.make_async_copy(
                    qkv_hbm.at[:, pl.ds(part * D + start * HD, (stop - start) * HD)],
                    qkv.at[part, :, pl.ds(start * HD, (stop - start) * HD)],
                    in_sem.at[8 + len(loads)],
                )
            )
    for load in small:
        load.start()

    barrier = pltpu.get_barrier_semaphore()
    for t in reversed(range(1, nc)):
        pl.semaphore_signal(barrier, inc=1, device_id=(peer(t),), device_id_type=MESH)
    pl.semaphore_signal(barrier, inc=1, device_id=(partner,), device_id_type=MESH)

    for load in loads:
        load.start()
    load_cache.start()
    load_weight.start()
    load_hidden.start()
    keep_weight.start()

    def start_chips(buf, x):
        for t in reversed(range(1, nc)):
            pltpu.make_async_remote_copy(
                src_ref=buf.at[core, chip],
                dst_ref=buf.at[core, chip],
                send_sem=chip_sem.at[2 * x],
                recv_sem=chip_sem.at[2 * x + 1],
                device_id=(peer(t),),
                device_id_type=MESH,
            ).start()

    def all_chips(buf, x):
        blocks = buf.at[core, pl.ds(0, nc - 1)]
        return pltpu.make_async_remote_copy(
            src_ref=blocks,
            dst_ref=blocks,
            send_sem=chip_sem.at[2 * x],
            recv_sem=chip_sem.at[2 * x + 1],
            device_id=(partner,),
            device_id_type=MESH,
        )

    def pair_copy(src, dst, x):
        return pltpu.make_async_remote_copy(
            src_ref=src,
            dst_ref=dst,
            send_sem=pair_sem.at[2 * x],
            recv_sem=pair_sem.at[2 * x + 1],
            device_id=(partner,),
            device_id_type=MESH,
        )

    tell = [
        pair_copy(where_hbm, pair_where, 0),
        pair_copy(owner_hbm, pair_owners, 1),
    ]

    def wanted(table, at):
        places = first_two([table[j] // RD != at for j in range(RD)])
        return [(place, table[jnp.maximum(place, 0)]) for place in places]

    def forward(buf, table):
        rows = []
        for place, item in wanted(table, partner):
            device = item // RD
            row = pick_marked(buf[core, device // 2], item % RD)
            here = jnp.logical_and(place >= 0, device % 2 == core)
            rows.append(jnp.where(here, row, 0.0))
        return rows

    def far_rows(buf, relay, table):
        passed = relay[1].astype(F32)
        rows = []
        for i, (place, item) in enumerate(wanted(table, me)):
            device = item // RD
            row = pick_marked(buf[core, device // 2], item % RD)
            rows.append(jnp.where(device % 2 == core, row, passed[i : i + 1]))
        return rows

    def segment(g):
        for load in loads[3 * g : 3 * g + 3]:
            load.wait()
        start, stop = CUTS[g]

        attend(start, stop, qkv, att)

    for load in small:
        load.wait()
    own = head_mask()
    mine = first[...].astype(F32)[:8]
    places = first_two([where[j] // RD != me for j in range(RD)])
    no_stats = jnp.zeros((1, HD), F32)
    qg[core, chip] = message(
        [jnp.concatenate([pick_row(mine[:, :D], j), no_stats], axis=1) for j in places], places
    )
    segment(0)
    pl.semaphore_wait(barrier, nc)
    start_chips(qg, 0)
    for copy in tell:
        copy.start()
    segment(1)
    segment(2)
    for copy in tell:
        copy.wait_recv()
    all_chips(qg, 0).wait_recv()
    relay_q[0] = two_rows(forward(qg, pair_owners))
    pass_q = pair_copy(relay_q.at[0], relay_q.at[1], 2)
    pass_q.start()
    load_cache.wait()
    row8 = lax.broadcasted_iota(jnp.int32, (8, EXT), 0)
    held = jnp.zeros((8, EXT), F32)
    parts = partials(
        [mine[j : j + 1, :D] for j in range(RD)],
        [where[j] % RD for j in range(RD)],
        cache,
        lengths,
        own,
    )
    for j, part in enumerate(parts):
        held = jnp.where(row8 == j, part, held)
    local_part[...] = held
    pass_q.wait_recv()

    places = first_two([owners[s] // RD != me for s in range(RD)])
    rows = partials(
        [q[:, :D] for q in far_rows(qg, relay_q, owners)],
        [jnp.maximum(place, 0) for place in places],
        cache,
        lengths,
        own,
    )
    cg[core, chip] = message(rows, places)

    start_chips(cg, 1)
    load_weight.wait()
    load_hidden.wait()
    is_prefill = flag[0] == 1

    flags[...] = jnp.full((8, HD), flag[0], jnp.int32).astype(F32)
    keep_flag = pltpu.make_async_copy(flags, flag_any, out_sem.at[1])
    keep_flag.start()
    keep_att = pltpu.make_async_copy(
        att.at[pl.ds(H, UP - H), :], att_any.at[pl.ds(H, UP - H), :], out_sem.at[2]
    )
    keep_att.start()

    def project(first_col, last_col):
        @pl.loop(first_col // NT, last_col // NT)
        def _(n):
            cols = pl.ds(pl.multiple_of(n * NT, NT), NT)
            rows = pl.ds(UP, TOK_DEV - UP)
            acc = jnp.dot(att[rows, :], weight[:, cols], preferred_element_type=F32)
            acc = jnp.where(is_prefill, acc, 0.0).astype(BF16).astype(F32)
            low[:, cols] = (hidden[:, cols].astype(F32) + acc).astype(BF16)

    own_scores = []
    for j in range(RD):
        product = mine[j : j + 1, :D] * mine[j : j + 1, D : 2 * D]
        own_scores.append(
            jnp.sum(jnp.where(own, product, 0.0), axis=1, keepdims=True) * SCALE
        )

    project(0, SPLIT)
    all_chips(cg, 1).wait_recv()
    relay_c[0] = two_rows(forward(cg, pair_where))
    pass_c = pair_copy(relay_c.at[0], relay_c.at[1], 3)
    pass_c.start()
    project(SPLIT, D)
    keep_low = pltpu.make_async_copy(low, low_any, out_sem.at[3])
    keep_low.start()
    pass_c.wait_recv()

    row16 = lax.broadcasted_iota(jnp.int32, (H, D), 0)
    row_h = lax.broadcasted_iota(jnp.int32, (H, HD), 0)
    lane_h = lax.broadcasted_iota(jnp.int32, (H, HD), 1)
    diagonal = lane_h % H == row_h
    is_max = jnp.logical_and(diagonal, lane_h < 3 * H)
    is_total = jnp.logical_and(
        diagonal, jnp.logical_and(lane_h >= 3 * H, lane_h < 6 * H)
    )
    decoded = jnp.zeros((H, D), F32)
    places = first_two([where[j] // RD != me for j in range(RD)])
    fars = far_rows(cg, relay_c, where)
    for j in range(RD):
        part = jnp.where(places[0] == j, fars[0], local_part[j : j + 1, :])
        part = jnp.where(places[1] == j, fars[1], part)
        co = part[:, :D]
        cm = jnp.sum(jnp.where(is_max, part[:, D:], 0.0), axis=1, keepdims=True)
        cl = jnp.sum(jnp.where(is_total, part[:, D:], 0.0), axis=1, keepdims=True)
        row = mine[j : j + 1]
        ns = own_scores[j]
        joint = jnp.maximum(cm, ns)
        wc = jnp.exp(cm - joint)
        wo = jnp.exp(ns - joint)
        whole = cl * wc + wo
        mixed = co * (wc / whole) + row[:, 2 * D :] * (wo / whole)
        decoded = jnp.where(
            row16 == j, jnp.sum(jnp.where(own, mixed, 0.0), axis=0, keepdims=True), decoded
        )
    kept = jnp.where(is_prefill, att[pl.ds(0, H), :].astype(F32), decoded)
    att[pl.ds(0, H), :] = kept.astype(BF16)
    keep_top = pltpu.make_async_copy(
        att.at[pl.ds(0, H), :], att_any.at[pl.ds(0, H), :], out_sem.at[4]
    )
    keep_top.start()
    all_chips(qg, 0).wait_send()
    all_chips(cg, 1).wait_send()
    for copy in [*tell, pass_q, pass_c]:
        copy.wait_send()
    keep_weight.wait()
    keep_flag.wait()
    keep_att.wait()
    keep_low.wait()
    keep_top.wait()


def finish(flag, att, low, weight, hidden, out_hbm, out, sem):
    is_prefill = jnp.max(flag[...]) > 0.5
    store_low = pltpu.make_async_copy(low, out_hbm.at[pl.ds(UP, TOK_DEV - UP), :], sem.at[0])
    store_low.start()

    def project(rows, n):
        cols = pl.ds(n * COLS, COLS)
        acc = jnp.dot(att[pl.ds(0, rows), :], weight[:, cols], preferred_element_type=F32)
        acc = acc.astype(BF16).astype(F32)
        out[pl.ds(0, rows), cols] = (hidden[pl.ds(0, rows), cols].astype(F32) + acc).astype(BF16)
        store = pltpu.make_async_copy(
            out.at[pl.ds(0, rows), cols], out_hbm.at[pl.ds(0, rows), cols], sem.at[2 + n]
        )
        store.start()
        return store

    @pl.when(is_prefill)
    def _():
        for store in [project(UP, n) for n in range(D // COLS)]:
            store.wait()

    @pl.when(jnp.logical_not(is_prefill))
    def _():
        rest = pl.ds(H, UP - H)
        store_rest = pltpu.make_async_copy(hidden.at[rest, :], out_hbm.at[rest, :], sem.at[1])
        store_rest.start()
        for store in [project(H, n) for n in range(D // COLS)]:
            store.wait()
        store_rest.wait()

    store_low.wait()


def local(hidden_in, qkv, cache, lengths, prefill_flag, cache_slot, slot_owner, out_weight, n):
    nc = n // 2
    hbm = pl.BlockSpec(memory_space=pltpu.HBM)
    dma = pltpu.SemaphoreType.DMA
    vmem = pl.BlockSpec(memory_space=pltpu.VMEM)
    keep = [
        jax.ShapeDtypeStruct((8, HD), F32),
        jax.ShapeDtypeStruct((UP, D), BF16),
        jax.ShapeDtypeStruct((TOK_DEV - UP, D), BF16),
        jax.ShapeDtypeStruct((D, D), BF16),
    ]
    args = [
        x if x.shape == (1,) else pltpu.with_memory_space_constraint(x, pltpu.HBM)
        for x in (lengths, prefill_flag, cache_slot, slot_owner, hidden_in, qkv, cache, out_weight)
    ]
    kept = pl.pallas_call(
        functools.partial(kernel, nc),
        out_shape=keep,
        in_specs=[hbm, pl.BlockSpec(memory_space=pltpu.SMEM)] + [hbm] * 6,
        out_specs=[pl.BlockSpec(memory_space=pl.ANY)] * 4,
        scratch_shapes=[
            pltpu.SMEM((RD,), jnp.int32),
            pltpu.SMEM((RD,), jnp.int32),
            pltpu.SMEM((RD,), jnp.int32),
            pltpu.SMEM((RD,), jnp.int32),
            pltpu.SMEM((RD,), jnp.int32),
            pltpu.VMEM((16, 3 * D), BF16),
            pltpu.VMEM((TOK_DEV - UP, D), BF16),
            pltpu.VMEM((3, TOK_DEV, D), BF16),
            pltpu.VMEM((RD, LMAX, 2 * D), BF16),
            pltpu.VMEM((D, D), BF16),
            pltpu.VMEM((TOK_DEV, D), BF16),
            pltpu.VMEM((TOK_DEV - UP, D), BF16),
            pltpu.VMEM((8, HD), F32),
            pltpu.VMEM((8, EXT), F32),
            pltpu.VMEM((2, nc, 2, EXT), BF16),
            pltpu.VMEM((2, nc, 2, EXT), BF16),
            pltpu.VMEM((2, 2, EXT), BF16),
            pltpu.VMEM((2, 2, EXT), BF16),
            dma((8 + 3 * len(CUTS),)),
            dma((5,)),
            dma((4,)),
            dma((8,)),
        ],
        compiler_params=pltpu.CompilerParams(
            collective_id=0, has_side_effects=True, vmem_limit_bytes=34 * 1024 * 1024
        ),
    )(*args)
    return pl.pallas_call(
        finish,
        out_shape=jax.ShapeDtypeStruct((TOK_DEV, D), BF16),
        in_specs=[vmem] * 5,
        out_specs=hbm,
        scratch_shapes=[pltpu.VMEM((UP, D), BF16), dma((2 + D // COLS,))],
        compiler_params=pltpu.CompilerParams(vmem_limit_bytes=34 * 1024 * 1024),
    )(*kept, hidden_in)


def solution(mesh):
    placed = (
        P("req", None),
        P("req", None),
        P("req", None, None),
        P("req"),
        P("req"),
        P("req"),
        P("req"),
        P(),
    )
    return jax.shard_map(
        functools.partial(local, n=mesh.shape["req"]),
        mesh=mesh,
        in_specs=placed,
        out_specs=P("req", None),
        check_vma=False,
    )
```

```python
import functools
import math

import jax
import jax.numpy as jnp
from jax import lax
from jax.experimental import pallas as pl
from jax.experimental.pallas import tpu as pltpu
from jax.sharding import PartitionSpec as P

D = 2048
H = 16
HD = 128
TOK_DEV = 512
RD = 4
LMAX = 128
HALF = TOK_DEV // 2
CUTS = ((0, 3), (3, 9), (9, 16))
UP = 128
COLS = 512
NT = 512
SPLIT = 1536
EXT = D + 2 * HD
SCALE = 1.0 / math.sqrt(HD)
SCALE2 = SCALE * math.log2(math.e)
F32 = jnp.float32
BF16 = jnp.bfloat16
MESH = pl.DeviceIdType.MESH
NEG = float(jnp.finfo(jnp.float32).min)


def score(x, y):
    return lax.dot_general(x, y, (((1,), (1,)), ((), ())), preferred_element_type=F32)


def head_scores(h, qkv):
    q = qkv[0, :, pl.ds(h * HD, HD)]
    keys = qkv[1, :, pl.ds(h * HD, HD)]
    return score(q, keys[:HALF]), score(q[HALF:], keys[HALF:])


def head_weights(scores):
    s_first, s_last = scores
    row = lax.broadcasted_iota(jnp.int32, (HALF, HALF), 0)
    lane = lax.broadcasted_iota(jnp.int32, (HALF, HALF), 1)
    causal = lane <= row
    s_last = jnp.where(causal, s_last, NEG)
    s_upper = jnp.where(causal, s_first[:HALF], NEG)
    s_lower = s_first[HALF:]
    top_upper = jnp.max(s_upper, axis=1, keepdims=True)
    top_lower = jnp.max(jnp.maximum(s_lower, s_last), axis=1, keepdims=True)
    return [
        jnp.exp2((s - top) * SCALE2).astype(BF16)
        for s, top in ((s_upper, top_upper), (s_lower, top_lower), (s_last, top_lower))
    ]


def head_values(h, weights, qkv, att):
    p_upper, p_lower, p_last = weights
    ones = jnp.ones((TOK_DEV, HD), BF16)
    values = jnp.concatenate([qkv[2, :, pl.ds(h * HD, HD)], ones], axis=1)
    lower = jnp.dot(
        jnp.concatenate([p_lower, p_last], axis=1), values, preferred_element_type=F32
    )
    upper = jnp.dot(p_upper, values[:HALF], preferred_element_type=F32)
    cols = pl.ds(h * HD, HD)
    att[pl.ds(0, HALF), cols] = (upper[:, :HD] / upper[:, HD:]).astype(BF16)
    att[pl.ds(HALF, HALF), cols] = (lower[:, :HD] / lower[:, HD:]).astype(BF16)


def attend(start, stop, qkv, att):
    scores = head_scores(start, qkv)
    for h in range(start, stop):
        later = head_scores(h + 1, qkv) if h + 1 < stop else None
        head_values(h, head_weights(scores), qkv, att)
        scores = later


def head_mask():
    row = lax.broadcasted_iota(jnp.int32, (H, D), 0)
    lane = lax.broadcasted_iota(jnp.int32, (H, D), 1)
    return (lane // HD) == row


def pick_row(block, j):
    row = lax.broadcasted_iota(jnp.int32, block.shape, 0)
    return jnp.sum(jnp.where(row == j, block.astype(F32), 0.0), axis=0, keepdims=True)


def pick_marked(block, place):
    block = block.astype(F32)
    wanted = block[:, D + HD :] == place.astype(F32)
    wanted = jnp.concatenate([wanted] * (EXT // HD), axis=1)
    return jnp.sum(jnp.where(wanted, block, 0.0), axis=0, keepdims=True)


def split3(x):
    pieces = []
    for _ in range(3):
        piece = x.astype(BF16).astype(F32)
        pieces.append(piece)
        x = x - piece
    return pieces


def first_two(far):
    one = jnp.int32(-1)
    two = jnp.int32(-1)
    for j in reversed(range(RD)):
        two = jnp.where(far[j], one, two)
        one = jnp.where(far[j], jnp.int32(j), one)
    return one, two


def two_rows(rows):
    row = lax.broadcasted_iota(jnp.int32, (2, EXT), 0)
    return jnp.where(row == 0, rows[0], rows[1]).astype(BF16)


def message(rows, places):
    lane = lax.broadcasted_iota(jnp.int32, (1, EXT), 1)
    marked = [
        jnp.where(lane >= D + HD, place.astype(F32), x) for x, place in zip(rows, places)
    ]
    return two_rows(marked)


def partials(queries, slots, cache, lengths, own):
    row = lax.broadcasted_iota(jnp.int32, (H, HD), 0)
    lane = lax.broadcasted_iota(jnp.int32, (H, HD), 1)
    scores = []
    for q, slot in zip(queries, slots):
        q_heads = jnp.where(own, q, 0.0).astype(BF16)
        scores.append(score(q_heads, cache[slot, :, pl.ds(0, D)]))
    weights = []
    for s, slot in zip(scores, slots):
        valid = lax.broadcasted_iota(jnp.int32, (H, LMAX), 1) < lengths[slot]
        s = jnp.where(valid, s, NEG)
        top = jnp.max(s, axis=1, keepdims=True)
        p = jnp.where(valid, jnp.exp2((s - top) * SCALE2), 0.0)
        weights.append((p.astype(BF16), top, jnp.sum(p, axis=1, keepdims=True)))
    sums = []
    for (p, _, _), slot in zip(weights, slots):
        o = jnp.dot(p, cache[slot, :, pl.ds(D, D)], preferred_element_type=F32)
        sums.append(jnp.sum(jnp.where(own, o, 0.0), axis=0, keepdims=True))
    parts = []
    for o, (_, top, total) in zip(sums, weights):
        stats = jnp.zeros((H, HD), F32)
        for k, piece in enumerate(split3(top * SCALE) + split3(total)):
            stats = jnp.where(lane == row + k * H, piece, stats)
        stats = jnp.sum(stats, axis=0, keepdims=True)
        parts.append(jnp.concatenate([o, stats, jnp.zeros((1, HD), F32)], axis=1))
    return parts


def kernel(
    nc,
    lengths_hbm,
    flag,
    where_hbm,
    owner_hbm,
    hidden_hbm,
    qkv_hbm,
    cache_hbm,
    weight_hbm,
    att,
    low,
    weight,
    lengths,
    where,
    owners,
    pair_where,
    pair_owners,
    first,
    hidden,
    qkv,
    cache,
    local_part,
    qg,
    cg,
    relay_q,
    relay_c,
    in_sem,
    chip_sem,
    pair_sem,
):
    me = lax.axis_index("req")
    chip = me // 2
    core = me % 2
    partner = chip * 2 + 1 - core

    def peer(i):
        return (i + jnp.where(i >= chip, 1, 0)) * 2 + core

    barrier = pltpu.get_barrier_semaphore()
    for t in range(nc - 1):
        pl.semaphore_signal(barrier, inc=1, device_id=(peer(t),), device_id_type=MESH)
    pl.semaphore_signal(barrier, inc=1, device_id=(partner,), device_id_type=MESH)

    small = [
        pltpu.make_async_copy(src, dst, in_sem.at[i])
        for i, (src, dst) in enumerate(
            [
                (where_hbm, where),
                (owner_hbm, owners),
                (lengths_hbm, lengths),
                (qkv_hbm.at[pl.ds(0, 16), :], first),
            ]
        )
    ]
    load_cache = pltpu.make_async_copy(cache_hbm, cache, in_sem.at[5])
    load_weight = pltpu.make_async_copy(weight_hbm, weight, in_sem.at[6])
    load_hidden = pltpu.make_async_copy(hidden_hbm.at[pl.ds(UP, TOK_DEV - UP), :], hidden, in_sem.at[7])
    loads = []
    for start, stop in CUTS:
        for part in range(3):
            loads.append(
                pltpu.make_async_copy(
                    qkv_hbm.at[:, pl.ds(part * D + start * HD, (stop - start) * HD)],
                    qkv.at[part, :, pl.ds(start * HD, (stop - start) * HD)],
                    in_sem.at[8 + len(loads)],
                )
            )
    for load in small:
        load.start()

    for load in loads:
        load.start()
    load_cache.start()
    load_weight.start()
    load_hidden.start()

    def start_chips(buf, x, order):
        for t in order:
            pltpu.make_async_remote_copy(
                src_ref=buf.at[core, chip],
                dst_ref=buf.at[core, chip],
                send_sem=chip_sem.at[2 * x],
                recv_sem=chip_sem.at[2 * x + 1],
                device_id=(peer(t),),
                device_id_type=MESH,
            ).start()

    def all_chips(buf, x):
        blocks = buf.at[core, pl.ds(0, nc - 1)]
        return pltpu.make_async_remote_copy(
            src_ref=blocks,
            dst_ref=blocks,
            send_sem=chip_sem.at[2 * x],
            recv_sem=chip_sem.at[2 * x + 1],
            device_id=(partner,),
            device_id_type=MESH,
        )

    def pair_copy(src, dst, x):
        return pltpu.make_async_remote_copy(
            src_ref=src,
            dst_ref=dst,
            send_sem=pair_sem.at[2 * x],
            recv_sem=pair_sem.at[2 * x + 1],
            device_id=(partner,),
            device_id_type=MESH,
        )

    tell = [
        pair_copy(where_hbm, pair_where, 0),
        pair_copy(owner_hbm, pair_owners, 1),
    ]

    def wanted(table, at):
        places = first_two([table[j] // RD != at for j in range(RD)])
        return [(place, table[jnp.maximum(place, 0)]) for place in places]

    def forward(buf, table):
        rows = []
        for place, item in wanted(table, partner):
            device = item // RD
            row = pick_marked(buf[core, device // 2], item % RD)
            here = jnp.logical_and(place >= 0, device % 2 == core)
            rows.append(jnp.where(here, row, 0.0))
        return rows

    def far_rows(buf, relay, table):
        passed = relay[1].astype(F32)
        rows = []
        for i, (place, item) in enumerate(wanted(table, me)):
            device = item // RD
            row = pick_marked(buf[core, device // 2], item % RD)
            rows.append(jnp.where(device % 2 == core, row, passed[i : i + 1]))
        return rows

    def segment(g):
        for load in loads[3 * g : 3 * g + 3]:
            load.wait()
        start, stop = CUTS[g]

        attend(start, stop, qkv, att)

    for load in small:
        load.wait()
    own = head_mask()
    mine = first[...].astype(F32)[:8]
    places = first_two([where[j] // RD != me for j in range(RD)])
    no_stats = jnp.zeros((1, 2 * HD), F32)
    qg[core, chip] = message(
        [jnp.concatenate([pick_row(mine[:, :D], j), no_stats], axis=1) for j in places], places
    )
    pl.semaphore_wait(barrier, nc)
    start_chips(qg, 0, reversed(range(nc - 1)))
    for copy in tell:
        copy.start()
    segment(0)
    segment(1)
    segment(2)
    for copy in tell:
        copy.wait_recv()
    all_chips(qg, 0).wait_recv()
    relay_q[0] = two_rows(forward(qg, pair_owners))
    pass_q = pair_copy(relay_q.at[0], relay_q.at[1], 2)
    pass_q.start()
    load_cache.wait()
    row8 = lax.broadcasted_iota(jnp.int32, (8, EXT), 0)
    held = jnp.zeros((8, EXT), F32)
    parts = partials(
        [mine[j : j + 1, :D] for j in range(RD)],
        [where[j] % RD for j in range(RD)],
        cache,
        lengths,
        own,
    )
    for j, part in enumerate(parts):
        held = jnp.where(row8 == j, part, held)
    local_part[...] = held
    pass_q.wait_recv()

    places = first_two([owners[s] // RD != me for s in range(RD)])
    rows = partials(
        [q[:, :D] for q in far_rows(qg, relay_q, owners)],
        [jnp.maximum(place, 0) for place in places],
        cache,
        lengths,
        own,
    )
    cg[core, chip] = message(rows, places)

    start_chips(cg, 1, range(nc - 1))
    load_weight.wait()
    load_hidden.wait()
    is_prefill = flag[0] == 1

    def project(first_col, last_col):
        @pl.loop(first_col // NT, last_col // NT)
        def _(n):
            cols = pl.ds(pl.multiple_of(n * NT, NT), NT)
            rows = pl.ds(UP, TOK_DEV - UP)
            acc = jnp.dot(att[rows, :], weight[:, cols], preferred_element_type=F32)
            acc = jnp.where(is_prefill, acc, 0.0).astype(BF16).astype(F32)
            low[:, cols] = (hidden[:, cols].astype(F32) + acc).astype(BF16)

    own_scores = []
    for j in range(RD):
        product = mine[j : j + 1, :D] * mine[j : j + 1, D : 2 * D]
        own_scores.append(
            jnp.sum(jnp.where(own, product, 0.0), axis=1, keepdims=True) * SCALE
        )

    project(0, SPLIT)
    all_chips(cg, 1).wait_recv()
    relay_c[0] = two_rows(forward(cg, pair_where))
    pass_c = pair_copy(relay_c.at[0], relay_c.at[1], 3)
    pass_c.start()
    project(SPLIT, D)
    pass_c.wait_recv()

    row16 = lax.broadcasted_iota(jnp.int32, (H, D), 0)
    row_h = lax.broadcasted_iota(jnp.int32, (H, HD), 0)
    lane_h = lax.broadcasted_iota(jnp.int32, (H, HD), 1)
    diagonal = lane_h % H == row_h
    is_max = jnp.logical_and(diagonal, lane_h < 3 * H)
    is_total = jnp.logical_and(
        diagonal, jnp.logical_and(lane_h >= 3 * H, lane_h < 6 * H)
    )
    decoded = jnp.zeros((H, D), F32)
    places = first_two([where[j] // RD != me for j in range(RD)])
    fars = far_rows(cg, relay_c, where)
    for j in range(RD):
        part = jnp.where(places[0] == j, fars[0], local_part[j : j + 1, :])
        part = jnp.where(places[1] == j, fars[1], part)
        co = part[:, :D]
        cm = jnp.sum(jnp.where(is_max, part[:, D : D + HD], 0.0), axis=1, keepdims=True)
        cl = jnp.sum(jnp.where(is_total, part[:, D : D + HD], 0.0), axis=1, keepdims=True)
        row = mine[j : j + 1]
        ns = own_scores[j]
        joint = jnp.maximum(cm, ns)
        wc = jnp.exp(cm - joint)
        wo = jnp.exp(ns - joint)
        whole = cl * wc + wo
        mixed = co * (wc / whole) + row[:, 2 * D :] * (wo / whole)
        decoded = jnp.where(
            row16 == j, jnp.sum(jnp.where(own, mixed, 0.0), axis=0, keepdims=True), decoded
        )
    kept = jnp.where(is_prefill, att[pl.ds(0, H), :].astype(F32), decoded)
    att[pl.ds(0, H), :] = kept.astype(BF16)
    all_chips(qg, 0).wait_send()
    all_chips(cg, 1).wait_send()
    for copy in [*tell, pass_q, pass_c]:
        copy.wait_send()


def finish(flag, att, low, weight, hidden, out_hbm, out, sem):
    is_prefill = flag[0] == 1
    store_low = pltpu.make_async_copy(low, out_hbm.at[pl.ds(UP, TOK_DEV - UP), :], sem.at[0])
    store_low.start()

    def project(rows, n):
        cols = pl.ds(n * COLS, COLS)
        acc = jnp.dot(att[pl.ds(0, rows), :], weight[:, cols], preferred_element_type=F32)
        acc = acc.astype(BF16).astype(F32)
        out[pl.ds(0, rows), cols] = (hidden[pl.ds(0, rows), cols].astype(F32) + acc).astype(BF16)
        store = pltpu.make_async_copy(
            out.at[pl.ds(0, rows), cols], out_hbm.at[pl.ds(0, rows), cols], sem.at[2 + n]
        )
        store.start()
        return store

    @pl.when(is_prefill)
    def _():
        for store in [project(UP, n) for n in range(D // COLS)]:
            store.wait()

    @pl.when(jnp.logical_not(is_prefill))
    def _():
        rest = pl.ds(H, UP - H)
        store_rest = pltpu.make_async_copy(hidden.at[rest, :], out_hbm.at[rest, :], sem.at[1])
        store_rest.start()
        for store in [project(H, n) for n in range(D // COLS)]:
            store.wait()
        store_rest.wait()

    store_low.wait()


def local(hidden_in, qkv, cache, lengths, prefill_flag, cache_slot, slot_owner, out_weight, n):
    nc = n // 2
    hbm = pl.BlockSpec(memory_space=pltpu.HBM)
    dma = pltpu.SemaphoreType.DMA
    vmem = pl.BlockSpec(memory_space=pltpu.VMEM)
    keep = [
        jax.ShapeDtypeStruct((TOK_DEV, D), BF16),
        jax.ShapeDtypeStruct((TOK_DEV - UP, D), BF16),
        jax.ShapeDtypeStruct((D, D), BF16),
    ]
    args = [
        x if x.shape == (1,) else pltpu.with_memory_space_constraint(x, pltpu.HBM)
        for x in (lengths, prefill_flag, cache_slot, slot_owner, hidden_in, qkv, cache, out_weight)
    ]
    kept = pl.pallas_call(
        functools.partial(kernel, nc),
        out_shape=keep,
        in_specs=[hbm, pl.BlockSpec(memory_space=pltpu.SMEM)] + [hbm] * 6,
        out_specs=[vmem] * 3,
        scratch_shapes=[
            pltpu.SMEM((RD,), jnp.int32),
            pltpu.SMEM((RD,), jnp.int32),
            pltpu.SMEM((RD,), jnp.int32),
            pltpu.SMEM((RD,), jnp.int32),
            pltpu.SMEM((RD,), jnp.int32),
            pltpu.VMEM((16, 3 * D), BF16),
            pltpu.VMEM((TOK_DEV - UP, D), BF16),
            pltpu.VMEM((3, TOK_DEV, D), BF16),
            pltpu.VMEM((RD, LMAX, 2 * D), BF16),
            pltpu.VMEM((8, EXT), F32),
            pltpu.VMEM((2, nc, 2, EXT), BF16),
            pltpu.VMEM((2, nc, 2, EXT), BF16),
            pltpu.VMEM((2, 2, EXT), BF16),
            pltpu.VMEM((2, 2, EXT), BF16),
            dma((8 + 3 * len(CUTS),)),
            dma((4,)),
            dma((8,)),
        ],
        compiler_params=pltpu.CompilerParams(
            collective_id=0, has_side_effects=True, vmem_limit_bytes=34 * 1024 * 1024
        ),
    )(*args)
    return pl.pallas_call(
        finish,
        out_shape=jax.ShapeDtypeStruct((TOK_DEV, D), BF16),
        in_specs=[pl.BlockSpec(memory_space=pltpu.SMEM)] + [vmem] * 4,
        out_specs=hbm,
        scratch_shapes=[pltpu.VMEM((UP, D), BF16), dma((2 + D // COLS,))],
        compiler_params=pltpu.CompilerParams(vmem_limit_bytes=34 * 1024 * 1024),
    )(prefill_flag, *kept, hidden_in)


def solution(mesh):
    placed = (
        P("req", None),
        P("req", None),
        P("req", None, None),
        P("req"),
        P("req"),
        P("req"),
        P("req"),
        P(),
    )
    return jax.shard_map(
        functools.partial(local, n=mesh.shape["req"]),
        mesh=mesh,
        in_specs=placed,
        out_specs=P("req", None),
        check_vma=False,
    )
```

```python
import functools
import math

import jax
import jax.numpy as jnp
from jax import lax
from jax.experimental import pallas as pl
from jax.experimental.pallas import tpu as pltpu
from jax.sharding import PartitionSpec as P

D = 2048
H = 16
HD = 128
TOK_DEV = 512
RD = 4
LMAX = 128
HALF = TOK_DEV // 2
CUTS = ((0, 3), (3, 9), (9, 16))
UP = 128
COLS = 512
NT = 512
EXT = D + 2 * HD
SCALE = 1.0 / math.sqrt(HD)
SCALE2 = SCALE * math.log2(math.e)
F32 = jnp.float32
BF16 = jnp.bfloat16
MESH = pl.DeviceIdType.MESH
NEG = float(jnp.finfo(jnp.float32).min)


def score(x, y):
    return lax.dot_general(x, y, (((1,), (1,)), ((), ())), preferred_element_type=F32)


def head_scores(h, qkv):
    q = qkv[0, :, pl.ds(h * HD, HD)]
    keys = qkv[1, :, pl.ds(h * HD, HD)]
    return score(q, keys[:HALF]), score(q[HALF:], keys[HALF:])


def head_weights(scores):
    s_first, s_last = scores
    row = lax.broadcasted_iota(jnp.int32, (HALF, HALF), 0)
    lane = lax.broadcasted_iota(jnp.int32, (HALF, HALF), 1)
    causal = lane <= row
    s_last = jnp.where(causal, s_last, NEG)
    s_upper = jnp.where(causal, s_first[:HALF], NEG)
    s_lower = s_first[HALF:]
    top_upper = jnp.max(s_upper, axis=1, keepdims=True)
    top_lower = jnp.max(jnp.maximum(s_lower, s_last), axis=1, keepdims=True)
    return [
        jnp.exp2((s - top) * SCALE2).astype(BF16)
        for s, top in ((s_upper, top_upper), (s_lower, top_lower), (s_last, top_lower))
    ]


def head_values(h, weights, qkv, att):
    p_upper, p_lower, p_last = weights
    ones = jnp.ones((TOK_DEV, HD), BF16)
    values = jnp.concatenate([qkv[2, :, pl.ds(h * HD, HD)], ones], axis=1)
    lower = jnp.dot(
        jnp.concatenate([p_lower, p_last], axis=1), values, preferred_element_type=F32
    )
    upper = jnp.dot(p_upper, values[:HALF], preferred_element_type=F32)
    cols = pl.ds(h * HD, HD)
    att[pl.ds(0, HALF), cols] = (upper[:, :HD] / upper[:, HD:]).astype(BF16)
    att[pl.ds(HALF, HALF), cols] = (lower[:, :HD] / lower[:, HD:]).astype(BF16)


def attend(start, stop, qkv, att):
    scores = head_scores(start, qkv)
    for h in range(start, stop):
        later = head_scores(h + 1, qkv) if h + 1 < stop else None
        head_values(h, head_weights(scores), qkv, att)
        scores = later


def head_mask():
    row = lax.broadcasted_iota(jnp.int32, (H, D), 0)
    lane = lax.broadcasted_iota(jnp.int32, (H, D), 1)
    return (lane // HD) == row


def pick_row(block, j):
    row = lax.broadcasted_iota(jnp.int32, block.shape, 0)
    return jnp.sum(jnp.where(row == j, block.astype(F32), 0.0), axis=0, keepdims=True)


def pick_marked(block, place):
    block = block.astype(F32)
    wanted = block[:, D + HD :] == place.astype(F32)
    wanted = jnp.concatenate([wanted] * (EXT // HD), axis=1)
    return jnp.sum(jnp.where(wanted, block, 0.0), axis=0, keepdims=True)


def split3(x):
    pieces = []
    for _ in range(3):
        piece = x.astype(BF16).astype(F32)
        pieces.append(piece)
        x = x - piece
    return pieces


def first_two(far):
    one = jnp.int32(-1)
    two = jnp.int32(-1)
    for j in reversed(range(RD)):
        two = jnp.where(far[j], one, two)
        one = jnp.where(far[j], jnp.int32(j), one)
    return one, two


def two_rows(rows):
    row = lax.broadcasted_iota(jnp.int32, (2, EXT), 0)
    return jnp.where(row == 0, rows[0], rows[1]).astype(BF16)


def message(rows, places):
    lane = lax.broadcasted_iota(jnp.int32, (1, EXT), 1)
    marked = [
        jnp.where(lane >= D + HD, place.astype(F32), x) for x, place in zip(rows, places)
    ]
    return two_rows(marked)


def partials(queries, slots, cache, lengths, own):
    row = lax.broadcasted_iota(jnp.int32, (H, HD), 0)
    lane = lax.broadcasted_iota(jnp.int32, (H, HD), 1)
    scores = []
    for q, slot in zip(queries, slots):
        q_heads = jnp.where(own, q, 0.0).astype(BF16)
        scores.append(score(q_heads, cache[slot, :, pl.ds(0, D)]))
    weights = []
    for s, slot in zip(scores, slots):
        valid = lax.broadcasted_iota(jnp.int32, (H, LMAX), 1) < lengths[slot]
        s = jnp.where(valid, s, NEG)
        top = jnp.max(s, axis=1, keepdims=True)
        p = jnp.where(valid, jnp.exp2((s - top) * SCALE2), 0.0)
        weights.append((p.astype(BF16), top, jnp.sum(p, axis=1, keepdims=True)))
    sums = []
    for (p, _, _), slot in zip(weights, slots):
        o = jnp.dot(p, cache[slot, :, pl.ds(D, D)], preferred_element_type=F32)
        sums.append(jnp.sum(jnp.where(own, o, 0.0), axis=0, keepdims=True))
    parts = []
    for o, (_, top, total) in zip(sums, weights):
        stats = jnp.zeros((H, HD), F32)
        for k, piece in enumerate(split3(top * SCALE) + split3(total)):
            stats = jnp.where(lane == row + k * H, piece, stats)
        stats = jnp.sum(stats, axis=0, keepdims=True)
        parts.append(jnp.concatenate([o, stats, jnp.zeros((1, HD), F32)], axis=1))
    return parts


def kernel(
    nc,
    lengths_hbm,
    flag,
    where_hbm,
    owner_hbm,
    hidden_hbm,
    qkv_hbm,
    cache_hbm,
    weight_hbm,
    att,
    low,
    weight,
    lengths,
    where,
    owners,
    pair_where,
    pair_owners,
    first,
    hidden,
    qkv,
    cache,
    local_part,
    qg,
    cg,
    relay_q,
    relay_c,
    in_sem,
    chip_sem,
    pair_sem,
):
    me = lax.axis_index("req")
    chip = me // 2
    core = me % 2
    partner = chip * 2 + 1 - core

    def peer(i):
        return (i + jnp.where(i >= chip, 1, 0)) * 2 + core

    def far_first(i):
        return peer(jnp.where(chip >= nc // 2, i, nc - 2 - i))

    barrier = pltpu.get_barrier_semaphore()
    for t in range(nc - 1):
        pl.semaphore_signal(barrier, inc=1, device_id=(peer(t),), device_id_type=MESH)
    pl.semaphore_signal(barrier, inc=1, device_id=(partner,), device_id_type=MESH)

    small = [
        pltpu.make_async_copy(src, dst, in_sem.at[i])
        for i, (src, dst) in enumerate(
            [
                (where_hbm, where),
                (owner_hbm, owners),
                (lengths_hbm, lengths),
                (qkv_hbm.at[pl.ds(0, 16), :], first),
            ]
        )
    ]
    load_cache = pltpu.make_async_copy(cache_hbm, cache, in_sem.at[5])
    load_weight = pltpu.make_async_copy(weight_hbm, weight, in_sem.at[6])
    load_hidden = pltpu.make_async_copy(hidden_hbm.at[pl.ds(UP, TOK_DEV - UP), :], hidden, in_sem.at[7])
    loads = []
    for start, stop in CUTS:
        for part in range(3):
            loads.append(
                pltpu.make_async_copy(
                    qkv_hbm.at[:, pl.ds(part * D + start * HD, (stop - start) * HD)],
                    qkv.at[part, :, pl.ds(start * HD, (stop - start) * HD)],
                    in_sem.at[8 + len(loads)],
                )
            )
    for load in small:
        load.start()

    for load in loads:
        load.start()
    load_cache.start()
    load_weight.start()
    load_hidden.start()

    def start_chips(buf, x, peers):
        for target in peers:
            pltpu.make_async_remote_copy(
                src_ref=buf.at[core, chip],
                dst_ref=buf.at[core, chip],
                send_sem=chip_sem.at[2 * x],
                recv_sem=chip_sem.at[2 * x + 1],
                device_id=(target,),
                device_id_type=MESH,
            ).start()

    def all_chips(buf, x):
        blocks = buf.at[core, pl.ds(0, nc - 1)]
        return pltpu.make_async_remote_copy(
            src_ref=blocks,
            dst_ref=blocks,
            send_sem=chip_sem.at[2 * x],
            recv_sem=chip_sem.at[2 * x + 1],
            device_id=(partner,),
            device_id_type=MESH,
        )

    def to_first(blocks):
        return pltpu.make_async_remote_copy(
            src_ref=blocks,
            dst_ref=blocks,
            send_sem=chip_sem.at[4],
            recv_sem=chip_sem.at[5],
            device_id=(1 - core,),
            device_id_type=MESH,
        )

    def pair_copy(src, dst, x):
        return pltpu.make_async_remote_copy(
            src_ref=src,
            dst_ref=dst,
            send_sem=pair_sem.at[2 * x],
            recv_sem=pair_sem.at[2 * x + 1],
            device_id=(partner,),
            device_id_type=MESH,
        )

    tell = [
        pair_copy(where_hbm, pair_where, 0),
        pair_copy(owner_hbm, pair_owners, 1),
    ]

    def wanted(table, at):
        places = first_two([table[j] // RD != at for j in range(RD)])
        found = []
        for place in places:
            item = table[jnp.maximum(place, 0)]
            device = item // RD
            here = jnp.logical_and(place >= 0, device % 2 == core)
            found.append((place, device // 2, item % RD, here))
        return found

    def forward(buf, found):
        return two_rows(
            [
                jnp.where(here, pick_marked(buf[core, at], index), 0.0)
                for _, at, index, here in found
            ]
        )

    def far_rows(buf, relay, found):
        passed = relay[1].astype(F32)
        return [
            jnp.where(here, pick_marked(buf[core, at], index), passed[i : i + 1])
            for i, (_, at, index, here) in enumerate(found)
        ]

    def segment(g):
        for load in loads[3 * g : 3 * g + 3]:
            load.wait()
        start, stop = CUTS[g]

        attend(start, stop, qkv, att)

    for load in small:
        load.wait()
    own = head_mask()
    mine = first[...].astype(F32)[:8]
    far_requests = wanted(where, me)
    far_slots = wanted(owners, me)
    places = [place for place, _, _, _ in far_requests]
    no_stats = jnp.zeros((1, 2 * HD), F32)
    qg[core, chip] = message(
        [jnp.concatenate([pick_row(mine[:, :D], j), no_stats], axis=1) for j in places], places
    )
    pl.semaphore_wait(barrier, nc)
    start_chips(qg, 0, [far_first(t) for t in range(nc - 1)])
    for copy in tell:
        copy.start()
    segment(0)
    segment(1)
    segment(2)
    for copy in tell:
        copy.wait_recv()
    pair_requests = wanted(pair_where, partner)
    pair_slots = wanted(pair_owners, partner)
    all_chips(qg, 0).wait_recv()
    relay_q[0] = forward(qg, pair_slots)
    pass_q = pair_copy(relay_q.at[0], relay_q.at[1], 2)
    pass_q.start()
    load_cache.wait()
    row8 = lax.broadcasted_iota(jnp.int32, (8, EXT), 0)
    held = jnp.zeros((8, EXT), F32)
    parts = partials(
        [mine[j : j + 1, :D] for j in range(RD)],
        [where[j] % RD for j in range(RD)],
        cache,
        lengths,
        own,
    )
    for j, part in enumerate(parts):
        held = jnp.where(row8 == j, part, held)
    local_part[...] = held
    pass_q.wait_recv()

    places = [place for place, _, _, _ in far_slots]
    rows = partials(
        [q[:, :D] for q in far_rows(qg, relay_q, far_slots)],
        [jnp.maximum(place, 0) for place in places],
        cache,
        lengths,
        own,
    )
    cg[core, chip] = message(rows, places)

    start_chips(cg, 1, [peer(0)])
    to_first(cg.at[core, chip]).start()
    start_chips(cg, 1, [peer(t) for t in range(1, nc - 1)])
    load_weight.wait()
    load_hidden.wait()
    is_prefill = flag[0] == 1

    own_scores = []
    for j in range(RD):
        product = mine[j : j + 1, :D] * mine[j : j + 1, D : 2 * D]
        own_scores.append(
            jnp.sum(jnp.where(own, product, 0.0), axis=1, keepdims=True) * SCALE
        )


    @pl.loop(0, D // NT)
    def _(n):
        cols = pl.ds(pl.multiple_of(n * NT, NT), NT)
        rows = pl.ds(UP, TOK_DEV - UP)
        acc = jnp.dot(att[rows, :], weight[:, cols], preferred_element_type=F32)
        acc = jnp.where(is_prefill, acc, 0.0).astype(BF16).astype(F32)
        low[:, cols] = (hidden[:, cols].astype(F32) + acc).astype(BF16)

    all_chips(cg, 1).wait_recv()
    pass_c = pair_copy(relay_c.at[0], relay_c.at[1], 3)

    @pl.when(chip > 0)
    def _():
        relay_c[0] = forward(cg, pair_requests)
        pass_c.start()
        pass_c.wait()

    @pl.when(chip == 0)
    def _():
        to_first(cg.at[1 - core]).wait_recv()
        relay_c[1] = two_rows(
            [pick_marked(cg[1 - core, at], index) for _, at, index, _ in far_requests]
        )


    row16 = lax.broadcasted_iota(jnp.int32, (H, D), 0)
    row_h = lax.broadcasted_iota(jnp.int32, (H, HD), 0)
    lane_h = lax.broadcasted_iota(jnp.int32, (H, HD), 1)
    diagonal = lane_h % H == row_h
    is_max = jnp.logical_and(diagonal, lane_h < 3 * H)
    is_total = jnp.logical_and(
        diagonal, jnp.logical_and(lane_h >= 3 * H, lane_h < 6 * H)
    )
    decoded = jnp.zeros((H, D), F32)
    places = [place for place, _, _, _ in far_requests]
    fars = far_rows(cg, relay_c, far_requests)
    for j in range(RD):
        part = jnp.where(places[0] == j, fars[0], local_part[j : j + 1, :])
        part = jnp.where(places[1] == j, fars[1], part)
        co = part[:, :D]
        cm = jnp.sum(jnp.where(is_max, part[:, D : D + HD], 0.0), axis=1, keepdims=True)
        cl = jnp.sum(jnp.where(is_total, part[:, D : D + HD], 0.0), axis=1, keepdims=True)
        row = mine[j : j + 1]
        ns = own_scores[j]
        joint = jnp.maximum(cm, ns)
        wc = jnp.exp(cm - joint)
        wo = jnp.exp(ns - joint)
        whole = cl * wc + wo
        mixed = co * (wc / whole) + row[:, 2 * D :] * (wo / whole)
        decoded = jnp.where(
            row16 == j, jnp.sum(jnp.where(own, mixed, 0.0), axis=0, keepdims=True), decoded
        )
    kept = jnp.where(is_prefill, att[pl.ds(0, H), :].astype(F32), decoded)
    att[pl.ds(0, H), :] = kept.astype(BF16)
    all_chips(qg, 0).wait_send()
    all_chips(cg, 1).wait_send()
    to_first(cg.at[core, chip]).wait_send()
    for copy in [*tell, pass_q]:
        copy.wait_send()


def finish(flag, att, low, weight, hidden, out_hbm, out, sem):
    is_prefill = flag[0] == 1
    store_low = pltpu.make_async_copy(low, out_hbm.at[pl.ds(UP, TOK_DEV - UP), :], sem.at[0])
    store_low.start()

    def project(rows, n):
        cols = pl.ds(n * COLS, COLS)
        acc = jnp.dot(att[pl.ds(0, rows), :], weight[:, cols], preferred_element_type=F32)
        acc = acc.astype(BF16).astype(F32)
        out[pl.ds(0, rows), cols] = (hidden[pl.ds(0, rows), cols].astype(F32) + acc).astype(BF16)
        store = pltpu.make_async_copy(
            out.at[pl.ds(0, rows), cols], out_hbm.at[pl.ds(0, rows), cols], sem.at[2 + n]
        )
        store.start()
        return store

    @pl.when(is_prefill)
    def _():
        for store in [project(UP, n) for n in range(D // COLS)]:
            store.wait()

    @pl.when(jnp.logical_not(is_prefill))
    def _():
        rest = pl.ds(H, UP - H)
        store_rest = pltpu.make_async_copy(hidden.at[rest, :], out_hbm.at[rest, :], sem.at[1])
        store_rest.start()
        for store in [project(H, n) for n in range(D // COLS)]:
            store.wait()
        store_rest.wait()

    store_low.wait()


def local(hidden_in, qkv, cache, lengths, prefill_flag, cache_slot, slot_owner, out_weight, n):
    nc = n // 2
    hbm = pl.BlockSpec(memory_space=pltpu.HBM)
    dma = pltpu.SemaphoreType.DMA
    vmem = pl.BlockSpec(memory_space=pltpu.VMEM)
    keep = [
        jax.ShapeDtypeStruct((TOK_DEV, D), BF16),
        jax.ShapeDtypeStruct((TOK_DEV - UP, D), BF16),
        jax.ShapeDtypeStruct((D, D), BF16),
    ]
    args = [
        x if x.shape == (1,) else pltpu.with_memory_space_constraint(x, pltpu.HBM)
        for x in (lengths, prefill_flag, cache_slot, slot_owner, hidden_in, qkv, cache, out_weight)
    ]
    kept = pl.pallas_call(
        functools.partial(kernel, nc),
        out_shape=keep,
        in_specs=[hbm, pl.BlockSpec(memory_space=pltpu.SMEM)] + [hbm] * 6,
        out_specs=[vmem] * 3,
        scratch_shapes=[
            pltpu.SMEM((RD,), jnp.int32),
            pltpu.SMEM((RD,), jnp.int32),
            pltpu.SMEM((RD,), jnp.int32),
            pltpu.SMEM((RD,), jnp.int32),
            pltpu.SMEM((RD,), jnp.int32),
            pltpu.VMEM((16, 3 * D), BF16),
            pltpu.VMEM((TOK_DEV - UP, D), BF16),
            pltpu.VMEM((3, TOK_DEV, D), BF16),
            pltpu.VMEM((RD, LMAX, 2 * D), BF16),
            pltpu.VMEM((8, EXT), F32),
            pltpu.VMEM((2, nc, 2, EXT), BF16),
            pltpu.VMEM((2, nc, 2, EXT), BF16),
            pltpu.VMEM((2, 2, EXT), BF16),
            pltpu.VMEM((2, 2, EXT), BF16),
            dma((8 + 3 * len(CUTS),)),
            dma((6,)),
            dma((8,)),
        ],
        compiler_params=pltpu.CompilerParams(
            collective_id=0, has_side_effects=True, vmem_limit_bytes=34 * 1024 * 1024
        ),
    )(*args)
    return pl.pallas_call(
        finish,
        out_shape=jax.ShapeDtypeStruct((TOK_DEV, D), BF16),
        in_specs=[pl.BlockSpec(memory_space=pltpu.SMEM)] + [vmem] * 4,
        out_specs=hbm,
        scratch_shapes=[pltpu.VMEM((UP, D), BF16), dma((2 + D // COLS,))],
        compiler_params=pltpu.CompilerParams(vmem_limit_bytes=34 * 1024 * 1024),
    )(prefill_flag, *kept, hidden_in)


def solution(mesh):
    placed = (
        P("req", None),
        P("req", None),
        P("req", None, None),
        P("req"),
        P("req"),
        P("req"),
        P("req"),
        P(),
    )
    return jax.shard_map(
        functools.partial(local, n=mesh.shape["req"]),
        mesh=mesh,
        in_specs=placed,
        out_specs=P("req", None),
        check_vma=False,
    )
```

```python
import functools
import math

import jax
import jax.numpy as jnp
from jax import lax
from jax.experimental import pallas as pl
from jax.experimental.pallas import tpu as pltpu
from jax.sharding import PartitionSpec as P

D = 2048
H = 16
HD = 128
TOK_DEV = 512
RD = 4
LMAX = 128
HALF = TOK_DEV // 2
CUTS = ((0, 3), (3, 9), (9, 16))
UP = 128
COLS = 512
NT = 512
EXT = D + 2 * HD
SCALE = 1.0 / math.sqrt(HD)
SCALE2 = SCALE * math.log2(math.e)
F32 = jnp.float32
BF16 = jnp.bfloat16
MESH = pl.DeviceIdType.MESH
NEG = float(jnp.finfo(jnp.float32).min)


def score(x, y):
    return lax.dot_general(x, y, (((1,), (1,)), ((), ())), preferred_element_type=F32)


def head_scores(h, qkv):
    q = qkv[0, :, pl.ds(h * HD, HD)]
    keys = qkv[1, :, pl.ds(h * HD, HD)]
    return score(q, keys[:HALF]), score(q[HALF:], keys[HALF:])


def head_weights(scores):
    s_first, s_last = scores
    row = lax.broadcasted_iota(jnp.int32, (HALF, HALF), 0)
    lane = lax.broadcasted_iota(jnp.int32, (HALF, HALF), 1)
    causal = lane <= row
    s_last = jnp.where(causal, s_last, NEG)
    s_upper = jnp.where(causal, s_first[:HALF], NEG)
    s_lower = s_first[HALF:]
    top_upper = jnp.max(s_upper, axis=1, keepdims=True)
    top_lower = jnp.max(jnp.maximum(s_lower, s_last), axis=1, keepdims=True)
    return [
        jnp.exp2((s - top) * SCALE2).astype(BF16)
        for s, top in ((s_upper, top_upper), (s_lower, top_lower), (s_last, top_lower))
    ]


def head_values(h, weights, qkv, att):
    p_upper, p_lower, p_last = weights
    ones = jnp.ones((TOK_DEV, HD), BF16)
    values = jnp.concatenate([qkv[2, :, pl.ds(h * HD, HD)], ones], axis=1)
    lower = jnp.dot(
        jnp.concatenate([p_lower, p_last], axis=1), values, preferred_element_type=F32
    )
    upper = jnp.dot(p_upper, values[:HALF], preferred_element_type=F32)
    cols = pl.ds(h * HD, HD)
    att[pl.ds(0, HALF), cols] = (upper[:, :HD] / upper[:, HD:]).astype(BF16)
    att[pl.ds(HALF, HALF), cols] = (lower[:, :HD] / lower[:, HD:]).astype(BF16)


def attend(start, stop, qkv, att):
    scores = head_scores(start, qkv)
    for h in range(start, stop):
        later = head_scores(h + 1, qkv) if h + 1 < stop else None
        head_values(h, head_weights(scores), qkv, att)
        scores = later


def head_mask():
    row = lax.broadcasted_iota(jnp.int32, (H, D), 0)
    lane = lax.broadcasted_iota(jnp.int32, (H, D), 1)
    return (lane // HD) == row


def pick_row(block, j):
    row = lax.broadcasted_iota(jnp.int32, block.shape, 0)
    return jnp.sum(jnp.where(row == j, block.astype(F32), 0.0), axis=0, keepdims=True)


def pick_marked(block, place):
    block = block.astype(F32)
    wanted = block[:, D + HD :] == place.astype(F32)
    wanted = jnp.concatenate([wanted] * (EXT // HD), axis=1)
    return jnp.sum(jnp.where(wanted, block, 0.0), axis=0, keepdims=True)


def split3(x):
    pieces = []
    for _ in range(3):
        piece = x.astype(BF16).astype(F32)
        pieces.append(piece)
        x = x - piece
    return pieces


def first_two(far):
    one = jnp.int32(-1)
    two = jnp.int32(-1)
    for j in reversed(range(RD)):
        two = jnp.where(far[j], one, two)
        one = jnp.where(far[j], jnp.int32(j), one)
    return one, two


def two_rows(rows):
    row = lax.broadcasted_iota(jnp.int32, (2, EXT), 0)
    return jnp.where(row == 0, rows[0], rows[1]).astype(BF16)


def message(rows, places):
    lane = lax.broadcasted_iota(jnp.int32, (1, EXT), 1)
    marked = [
        jnp.where(lane >= D + HD, place.astype(F32), x) for x, place in zip(rows, places)
    ]
    return two_rows(marked)


def partials(queries, slots, cache, lengths, own):
    row = lax.broadcasted_iota(jnp.int32, (H, HD), 0)
    lane = lax.broadcasted_iota(jnp.int32, (H, HD), 1)
    scores = []
    for q, slot in zip(queries, slots):
        q_heads = jnp.where(own, q, 0.0).astype(BF16)
        scores.append(score(q_heads, cache[slot, :, pl.ds(0, D)]))
    weights = []
    for s, slot in zip(scores, slots):
        valid = lax.broadcasted_iota(jnp.int32, (H, LMAX), 1) < lengths[slot]
        s = jnp.where(valid, s, NEG)
        top = jnp.max(s, axis=1, keepdims=True)
        p = jnp.where(valid, jnp.exp2((s - top) * SCALE2), 0.0)
        weights.append((p.astype(BF16), top, jnp.sum(p, axis=1, keepdims=True)))
    sums = []
    for (p, _, _), slot in zip(weights, slots):
        o = jnp.dot(p, cache[slot, :, pl.ds(D, D)], preferred_element_type=F32)
        sums.append(jnp.sum(jnp.where(own, o, 0.0), axis=0, keepdims=True))
    parts = []
    for o, (_, top, total) in zip(sums, weights):
        stats = jnp.zeros((H, HD), F32)
        for k, piece in enumerate(split3(top * SCALE) + split3(total)):
            stats = jnp.where(lane == row + k * H, piece, stats)
        stats = jnp.sum(stats, axis=0, keepdims=True)
        parts.append(jnp.concatenate([o, stats, jnp.zeros((1, HD), F32)], axis=1))
    return parts


def kernel(
    nc,
    lengths_hbm,
    flag,
    where_hbm,
    owner_hbm,
    hidden_hbm,
    qkv_hbm,
    cache_hbm,
    weight_hbm,
    att,
    low,
    weight,
    lengths,
    where,
    owners,
    pair_where,
    pair_owners,
    first,
    hidden,
    qkv,
    cache,
    local_part,
    qg,
    cg,
    relay_q,
    relay_c,
    in_sem,
    chip_sem,
    pair_sem,
):
    me = lax.axis_index("req")
    chip = me // 2
    core = me % 2
    partner = chip * 2 + 1 - core

    def peer(i):
        return (i + jnp.where(i >= chip, 1, 0)) * 2 + core

    def far_first(i):
        return peer(jnp.where(chip >= nc // 2, i, nc - 2 - i))

    barrier = pltpu.get_barrier_semaphore()
    for t in range(nc - 1):
        pl.semaphore_signal(barrier, inc=1, device_id=(peer(t),), device_id_type=MESH)
    pl.semaphore_signal(barrier, inc=1, device_id=(partner,), device_id_type=MESH)

    small = [
        pltpu.make_async_copy(src, dst, in_sem.at[i])
        for i, (src, dst) in enumerate(
            [
                (where_hbm, where),
                (owner_hbm, owners),
                (lengths_hbm, lengths),
                (qkv_hbm.at[pl.ds(0, 16), :], first),
            ]
        )
    ]
    load_cache = pltpu.make_async_copy(cache_hbm, cache, in_sem.at[5])
    load_weight = pltpu.make_async_copy(weight_hbm, weight, in_sem.at[6])
    load_hidden = pltpu.make_async_copy(hidden_hbm.at[pl.ds(UP, TOK_DEV - UP), :], hidden, in_sem.at[7])
    loads = []
    for start, stop in CUTS:
        for part in range(3):
            loads.append(
                pltpu.make_async_copy(
                    qkv_hbm.at[:, pl.ds(part * D + start * HD, (stop - start) * HD)],
                    qkv.at[part, :, pl.ds(start * HD, (stop - start) * HD)],
                    in_sem.at[8 + len(loads)],
                )
            )
    for load in small:
        load.start()

    for load in loads:
        load.start()
    load_cache.start()
    load_weight.start()
    load_hidden.start()

    def start_chips(buf, x, peers):
        for target in peers:
            pltpu.make_async_remote_copy(
                src_ref=buf.at[core, chip],
                dst_ref=buf.at[core, chip],
                send_sem=chip_sem.at[2 * x],
                recv_sem=chip_sem.at[2 * x + 1],
                device_id=(target,),
                device_id_type=MESH,
            ).start()

    def all_chips(buf, x):
        blocks = buf.at[core, pl.ds(0, nc - 1)]
        return pltpu.make_async_remote_copy(
            src_ref=blocks,
            dst_ref=blocks,
            send_sem=chip_sem.at[2 * x],
            recv_sem=chip_sem.at[2 * x + 1],
            device_id=(partner,),
            device_id_type=MESH,
        )

    def to_first(blocks):
        return pltpu.make_async_remote_copy(
            src_ref=blocks,
            dst_ref=blocks,
            send_sem=chip_sem.at[4],
            recv_sem=chip_sem.at[5],
            device_id=(1 - core,),
            device_id_type=MESH,
        )

    def pair_copy(src, dst, x):
        return pltpu.make_async_remote_copy(
            src_ref=src,
            dst_ref=dst,
            send_sem=pair_sem.at[2 * x],
            recv_sem=pair_sem.at[2 * x + 1],
            device_id=(partner,),
            device_id_type=MESH,
        )

    tell = [
        pair_copy(where_hbm, pair_where, 0),
        pair_copy(owner_hbm, pair_owners, 1),
    ]

    def wanted(table, at):
        places = first_two([table[j] // RD != at for j in range(RD)])
        found = []
        for place in places:
            item = table[jnp.maximum(place, 0)]
            device = item // RD
            here = jnp.logical_and(place >= 0, device % 2 == core)
            found.append((place, device // 2, item % RD, here))
        return found

    def forward(buf, found):
        return two_rows(
            [
                jnp.where(here, pick_marked(buf[core, at], index), 0.0)
                for _, at, index, here in found
            ]
        )

    def far_rows(buf, relay, found):
        passed = relay[1].astype(F32)
        return [
            jnp.where(here, pick_marked(buf[core, at], index), passed[i : i + 1])
            for i, (_, at, index, here) in enumerate(found)
        ]

    def segment(g):
        for load in loads[3 * g : 3 * g + 3]:
            load.wait()
        start, stop = CUTS[g]

        attend(start, stop, qkv, att)

    for load in small:
        load.wait()
    own = head_mask()
    mine = first[...].astype(F32)[:8]
    far_requests = wanted(where, me)
    far_slots = wanted(owners, me)
    places = [place for place, _, _, _ in far_requests]
    no_stats = jnp.zeros((1, 2 * HD), F32)
    qg[core, chip] = message(
        [jnp.concatenate([pick_row(mine[:, :D], j), no_stats], axis=1) for j in places], places
    )
    def attend_local():
        row8 = lax.broadcasted_iota(jnp.int32, (8, EXT), 0)
        held = jnp.zeros((8, EXT), F32)
        parts = partials(
            [mine[j : j + 1, :D] for j in range(RD)],
            [where[j] % RD for j in range(RD)],
            cache,
            lengths,
            own,
        )
        for j, part in enumerate(parts):
            held = jnp.where(row8 == j, part, held)
        local_part[...] = held

    pl.semaphore_wait(barrier, nc)
    start_chips(qg, 0, [far_first(t) for t in range(nc - 1)])
    for copy in tell:
        copy.start()
    segment(0)
    segment(1)
    segment(2)
    for copy in tell:
        copy.wait_recv()
    pair_requests = wanted(pair_where, partner)
    pair_slots = wanted(pair_owners, partner)
    all_chips(qg, 0).wait_recv()
    relay_q[0] = forward(qg, pair_slots)
    pass_q = pair_copy(relay_q.at[0], relay_q.at[1], 2)
    pass_q.start()
    load_cache.wait()
    pass_q.wait_recv()

    places = [place for place, _, _, _ in far_slots]
    rows = partials(
        [q[:, :D] for q in far_rows(qg, relay_q, far_slots)],
        [jnp.maximum(place, 0) for place in places],
        cache,
        lengths,
        own,
    )
    cg[core, chip] = message(rows, places)

    start_chips(cg, 1, [peer(0)])
    to_first(cg.at[core, chip]).start()
    start_chips(cg, 1, [peer(t) for t in range(1, nc - 1)])
    attend_local()
    load_weight.wait()
    load_hidden.wait()
    is_prefill = flag[0] == 1

    own_scores = []
    for j in range(RD):
        product = mine[j : j + 1, :D] * mine[j : j + 1, D : 2 * D]
        own_scores.append(
            jnp.sum(jnp.where(own, product, 0.0), axis=1, keepdims=True) * SCALE
        )


    @pl.loop(0, D // NT)
    def _(n):
        cols = pl.ds(pl.multiple_of(n * NT, NT), NT)
        rows = pl.ds(UP, TOK_DEV - UP)
        acc = jnp.dot(att[rows, :], weight[:, cols], preferred_element_type=F32)
        acc = jnp.where(is_prefill, acc, 0.0).astype(BF16).astype(F32)
        low[:, cols] = (hidden[:, cols].astype(F32) + acc).astype(BF16)

    all_chips(cg, 1).wait_recv()
    pass_c = pair_copy(relay_c.at[0], relay_c.at[1], 3)

    @pl.when(chip > 0)
    def _():
        relay_c[0] = forward(cg, pair_requests)
        pass_c.start()
        pass_c.wait()

    @pl.when(chip == 0)
    def _():
        to_first(cg.at[1 - core]).wait_recv()
        relay_c[1] = two_rows(
            [pick_marked(cg[1 - core, at], index) for _, at, index, _ in far_requests]
        )


    row16 = lax.broadcasted_iota(jnp.int32, (H, D), 0)
    row_h = lax.broadcasted_iota(jnp.int32, (H, HD), 0)
    lane_h = lax.broadcasted_iota(jnp.int32, (H, HD), 1)
    diagonal = lane_h % H == row_h
    is_max = jnp.logical_and(diagonal, lane_h < 3 * H)
    is_total = jnp.logical_and(
        diagonal, jnp.logical_and(lane_h >= 3 * H, lane_h < 6 * H)
    )
    decoded = jnp.zeros((H, D), F32)
    places = [place for place, _, _, _ in far_requests]
    fars = far_rows(cg, relay_c, far_requests)
    for j in range(RD):
        part = jnp.where(places[0] == j, fars[0], local_part[j : j + 1, :])
        part = jnp.where(places[1] == j, fars[1], part)
        co = part[:, :D]
        cm = jnp.sum(jnp.where(is_max, part[:, D : D + HD], 0.0), axis=1, keepdims=True)
        cl = jnp.sum(jnp.where(is_total, part[:, D : D + HD], 0.0), axis=1, keepdims=True)
        row = mine[j : j + 1]
        ns = own_scores[j]
        joint = jnp.maximum(cm, ns)
        wc = jnp.exp(cm - joint)
        wo = jnp.exp(ns - joint)
        whole = cl * wc + wo
        mixed = co * (wc / whole) + row[:, 2 * D :] * (wo / whole)
        decoded = jnp.where(
            row16 == j, jnp.sum(jnp.where(own, mixed, 0.0), axis=0, keepdims=True), decoded
        )
    kept = jnp.where(is_prefill, att[pl.ds(0, H), :].astype(F32), decoded)
    att[pl.ds(0, H), :] = kept.astype(BF16)
    all_chips(qg, 0).wait_send()
    all_chips(cg, 1).wait_send()
    to_first(cg.at[core, chip]).wait_send()
    for copy in [*tell, pass_q]:
        copy.wait_send()


def finish(flag, att, low, weight, hidden, out_hbm, out, sem):
    is_prefill = flag[0] == 1
    store_low = pltpu.make_async_copy(low, out_hbm.at[pl.ds(UP, TOK_DEV - UP), :], sem.at[0])
    store_low.start()

    def project(rows, n):
        cols = pl.ds(n * COLS, COLS)
        acc = jnp.dot(att[pl.ds(0, rows), :], weight[:, cols], preferred_element_type=F32)
        acc = acc.astype(BF16).astype(F32)
        out[pl.ds(0, rows), cols] = (hidden[pl.ds(0, rows), cols].astype(F32) + acc).astype(BF16)
        store = pltpu.make_async_copy(
            out.at[pl.ds(0, rows), cols], out_hbm.at[pl.ds(0, rows), cols], sem.at[2 + n]
        )
        store.start()
        return store

    @pl.when(is_prefill)
    def _():
        for store in [project(UP, n) for n in range(D // COLS)]:
            store.wait()

    @pl.when(jnp.logical_not(is_prefill))
    def _():
        rest = pl.ds(H, UP - H)
        store_rest = pltpu.make_async_copy(hidden.at[rest, :], out_hbm.at[rest, :], sem.at[1])
        store_rest.start()
        for store in [project(H, n) for n in range(D // COLS)]:
            store.wait()
        store_rest.wait()

    store_low.wait()


def local(hidden_in, qkv, cache, lengths, prefill_flag, cache_slot, slot_owner, out_weight, n):
    nc = n // 2
    hbm = pl.BlockSpec(memory_space=pltpu.HBM)
    dma = pltpu.SemaphoreType.DMA
    vmem = pl.BlockSpec(memory_space=pltpu.VMEM)
    keep = [
        jax.ShapeDtypeStruct((TOK_DEV, D), BF16),
        jax.ShapeDtypeStruct((TOK_DEV - UP, D), BF16),
        jax.ShapeDtypeStruct((D, D), BF16),
    ]
    args = [
        x if x.shape == (1,) else pltpu.with_memory_space_constraint(x, pltpu.HBM)
        for x in (lengths, prefill_flag, cache_slot, slot_owner, hidden_in, qkv, cache, out_weight)
    ]
    kept = pl.pallas_call(
        functools.partial(kernel, nc),
        out_shape=keep,
        in_specs=[hbm, pl.BlockSpec(memory_space=pltpu.SMEM)] + [hbm] * 6,
        out_specs=[vmem] * 3,
        scratch_shapes=[
            pltpu.SMEM((RD,), jnp.int32),
            pltpu.SMEM((RD,), jnp.int32),
            pltpu.SMEM((RD,), jnp.int32),
            pltpu.SMEM((RD,), jnp.int32),
            pltpu.SMEM((RD,), jnp.int32),
            pltpu.VMEM((16, 3 * D), BF16),
            pltpu.VMEM((TOK_DEV - UP, D), BF16),
            pltpu.VMEM((3, TOK_DEV, D), BF16),
            pltpu.VMEM((RD, LMAX, 2 * D), BF16),
            pltpu.VMEM((8, EXT), F32),
            pltpu.VMEM((2, nc, 2, EXT), BF16),
            pltpu.VMEM((2, nc, 2, EXT), BF16),
            pltpu.VMEM((2, 2, EXT), BF16),
            pltpu.VMEM((2, 2, EXT), BF16),
            dma((8 + 3 * len(CUTS),)),
            dma((6,)),
            dma((8,)),
        ],
        compiler_params=pltpu.CompilerParams(
            collective_id=0, has_side_effects=True, vmem_limit_bytes=34 * 1024 * 1024
        ),
    )(*args)
    return pl.pallas_call(
        finish,
        out_shape=jax.ShapeDtypeStruct((TOK_DEV, D), BF16),
        in_specs=[pl.BlockSpec(memory_space=pltpu.SMEM)] + [vmem] * 4,
        out_specs=hbm,
        scratch_shapes=[pltpu.VMEM((UP, D), BF16), dma((2 + D // COLS,))],
        compiler_params=pltpu.CompilerParams(vmem_limit_bytes=34 * 1024 * 1024),
    )(prefill_flag, *kept, hidden_in)


def solution(mesh):
    placed = (
        P("req", None),
        P("req", None),
        P("req", None, None),
        P("req"),
        P("req"),
        P("req"),
        P("req"),
        P(),
    )
    return jax.shard_map(
        functools.partial(local, n=mesh.shape["req"]),
        mesh=mesh,
        in_specs=placed,
        out_specs=P("req", None),
        check_vma=False,
    )
```

```python
import functools
import math

import jax
import jax.numpy as jnp
from jax import lax
from jax.experimental import pallas as pl
from jax.experimental.pallas import tpu as pltpu
from jax.sharding import PartitionSpec as P

D = 2048
H = 16
HD = 128
TOK_DEV = 512
RD = 4
LMAX = 128
HALF = TOK_DEV // 2
CUTS = ((0, 3), (3, 9), (9, 16))
UP = 128
COLS = 512
NT = 512
EXT = D + 2 * HD
SCALE = 1.0 / math.sqrt(HD)
SCALE2 = SCALE * math.log2(math.e)
F32 = jnp.float32
BF16 = jnp.bfloat16
MESH = pl.DeviceIdType.MESH
NEG = float(jnp.finfo(jnp.float32).min)


def score(x, y):
    return lax.dot_general(x, y, (((1,), (1,)), ((), ())), preferred_element_type=F32)


def head_scores(h, qkv):
    q = qkv[0, :, pl.ds(h * HD, HD)]
    keys = qkv[1, :, pl.ds(h * HD, HD)]
    return score(q, keys[:HALF]), score(q[HALF:], keys[HALF:])


def head_weights(scores):
    s_first, s_last = scores
    row = lax.broadcasted_iota(jnp.int32, (HALF, HALF), 0)
    lane = lax.broadcasted_iota(jnp.int32, (HALF, HALF), 1)
    causal = lane <= row
    s_last = jnp.where(causal, s_last, NEG)
    s_upper = jnp.where(causal, s_first[:HALF], NEG)
    s_lower = s_first[HALF:]
    top_upper = jnp.max(s_upper, axis=1, keepdims=True)
    top_lower = jnp.max(jnp.maximum(s_lower, s_last), axis=1, keepdims=True)
    return [
        jnp.exp2((s - top) * SCALE2).astype(BF16)
        for s, top in ((s_upper, top_upper), (s_lower, top_lower), (s_last, top_lower))
    ]


def head_values(h, weights, qkv, att):
    p_upper, p_lower, p_last = weights
    ones = jnp.ones((TOK_DEV, HD), BF16)
    values = jnp.concatenate([qkv[2, :, pl.ds(h * HD, HD)], ones], axis=1)
    lower = jnp.dot(
        jnp.concatenate([p_lower, p_last], axis=1), values, preferred_element_type=F32
    )
    upper = jnp.dot(p_upper, values[:HALF], preferred_element_type=F32)
    cols = pl.ds(h * HD, HD)
    att[pl.ds(0, HALF), cols] = (upper[:, :HD] / upper[:, HD:]).astype(BF16)
    att[pl.ds(HALF, HALF), cols] = (lower[:, :HD] / lower[:, HD:]).astype(BF16)


def attend(start, stop, qkv, att):
    scores = head_scores(start, qkv)
    for h in range(start, stop):
        later = head_scores(h + 1, qkv) if h + 1 < stop else None
        head_values(h, head_weights(scores), qkv, att)
        scores = later


def head_mask():
    row = lax.broadcasted_iota(jnp.int32, (H, D), 0)
    lane = lax.broadcasted_iota(jnp.int32, (H, D), 1)
    return (lane // HD) == row


def pick_row(block, j):
    row = lax.broadcasted_iota(jnp.int32, block.shape, 0)
    return jnp.sum(jnp.where(row == j, block.astype(F32), 0.0), axis=0, keepdims=True)


def pick_marked(block, place):
    block = block.astype(F32)
    wanted = block[:, D + HD :] == place.astype(F32)
    wanted = jnp.concatenate([wanted] * (EXT // HD), axis=1)
    return jnp.sum(jnp.where(wanted, block, 0.0), axis=0, keepdims=True)


def split3(x):
    pieces = []
    for _ in range(3):
        piece = x.astype(BF16).astype(F32)
        pieces.append(piece)
        x = x - piece
    return pieces


def first_two(far):
    one = jnp.int32(-1)
    two = jnp.int32(-1)
    for j in reversed(range(RD)):
        two = jnp.where(far[j], one, two)
        one = jnp.where(far[j], jnp.int32(j), one)
    return one, two


def two_rows(rows):
    row = lax.broadcasted_iota(jnp.int32, (2, EXT), 0)
    return jnp.where(row == 0, rows[0], rows[1]).astype(BF16)


def message(rows, places):
    lane = lax.broadcasted_iota(jnp.int32, (1, EXT), 1)
    marked = [
        jnp.where(lane >= D + HD, place.astype(F32), x) for x, place in zip(rows, places)
    ]
    return two_rows(marked)


def partials(queries, slots, cache, lengths, own):
    row = lax.broadcasted_iota(jnp.int32, (H, HD), 0)
    lane = lax.broadcasted_iota(jnp.int32, (H, HD), 1)
    scores = []
    for q, slot in zip(queries, slots):
        q_heads = jnp.where(own, q, 0.0).astype(BF16)
        scores.append(score(q_heads, cache[slot, :, pl.ds(0, D)]))
    weights = []
    for s, slot in zip(scores, slots):
        valid = lax.broadcasted_iota(jnp.int32, (H, LMAX), 1) < lengths[slot]
        s = jnp.where(valid, s, NEG)
        top = jnp.max(s, axis=1, keepdims=True)
        p = jnp.where(valid, jnp.exp2((s - top) * SCALE2), 0.0)
        weights.append((p.astype(BF16), top, jnp.sum(p, axis=1, keepdims=True)))
    sums = []
    for (p, _, _), slot in zip(weights, slots):
        o = jnp.dot(p, cache[slot, :, pl.ds(D, D)], preferred_element_type=F32)
        sums.append(jnp.sum(jnp.where(own, o, 0.0), axis=0, keepdims=True))
    parts = []
    for o, (_, top, total) in zip(sums, weights):
        stats = jnp.zeros((H, HD), F32)
        for k, piece in enumerate(split3(top * SCALE) + split3(total)):
            stats = jnp.where(lane == row + k * H, piece, stats)
        stats = jnp.sum(stats, axis=0, keepdims=True)
        parts.append(jnp.concatenate([o, stats, jnp.zeros((1, HD), F32)], axis=1))
    return parts


def kernel(
    nc,
    lengths_hbm,
    flag,
    where_hbm,
    owner_hbm,
    hidden_hbm,
    qkv_hbm,
    cache_hbm,
    weight_hbm,
    att,
    low,
    weight,
    lengths,
    where,
    owners,
    pair_where,
    pair_owners,
    first,
    hidden,
    qkv,
    cache,
    local_part,
    qg,
    cg,
    relay_q,
    relay_c,
    in_sem,
    chip_sem,
    pair_sem,
):
    me = lax.axis_index("req")
    chip = me // 2
    core = me % 2
    partner = chip * 2 + 1 - core

    def peer(i):
        return (i + jnp.where(i >= chip, 1, 0)) * 2 + core

    def far_first(i):
        return peer(jnp.where(chip >= nc // 2, i, nc - 2 - i))

    barrier = pltpu.get_barrier_semaphore()
    for t in range(nc - 1):
        pl.semaphore_signal(barrier, inc=1, device_id=(peer(t),), device_id_type=MESH)
    pl.semaphore_signal(barrier, inc=1, device_id=(partner,), device_id_type=MESH)

    small = [
        pltpu.make_async_copy(src, dst, in_sem.at[i])
        for i, (src, dst) in enumerate(
            [
                (where_hbm, where),
                (owner_hbm, owners),
                (lengths_hbm, lengths),
                (qkv_hbm.at[pl.ds(0, 16), :], first),
            ]
        )
    ]
    load_cache = pltpu.make_async_copy(cache_hbm, cache, in_sem.at[5])
    load_weight = pltpu.make_async_copy(weight_hbm, weight, in_sem.at[6])
    load_hidden = pltpu.make_async_copy(hidden_hbm.at[pl.ds(UP, TOK_DEV - UP), :], hidden, in_sem.at[7])
    loads = []
    for start, stop in CUTS:
        for part in range(3):
            loads.append(
                pltpu.make_async_copy(
                    qkv_hbm.at[:, pl.ds(part * D + start * HD, (stop - start) * HD)],
                    qkv.at[part, :, pl.ds(start * HD, (stop - start) * HD)],
                    in_sem.at[8 + len(loads)],
                )
            )
    for load in small:
        load.start()

    for load in loads:
        load.start()
    load_cache.start()
    load_weight.start()
    load_hidden.start()

    def start_chips(buf, x, peers):
        for target in peers:
            pltpu.make_async_remote_copy(
                src_ref=buf.at[core, chip],
                dst_ref=buf.at[core, chip],
                send_sem=chip_sem.at[2 * x],
                recv_sem=chip_sem.at[2 * x + 1],
                device_id=(target,),
                device_id_type=MESH,
            ).start()

    def all_chips(buf, x):
        blocks = buf.at[core, pl.ds(0, nc - 1)]
        return pltpu.make_async_remote_copy(
            src_ref=blocks,
            dst_ref=blocks,
            send_sem=chip_sem.at[2 * x],
            recv_sem=chip_sem.at[2 * x + 1],
            device_id=(partner,),
            device_id_type=MESH,
        )

    def to_first(blocks):
        return pltpu.make_async_remote_copy(
            src_ref=blocks,
            dst_ref=blocks,
            send_sem=chip_sem.at[4],
            recv_sem=chip_sem.at[5],
            device_id=(1 - core,),
            device_id_type=MESH,
        )

    def pair_copy(src, dst, x):
        return pltpu.make_async_remote_copy(
            src_ref=src,
            dst_ref=dst,
            send_sem=pair_sem.at[2 * x],
            recv_sem=pair_sem.at[2 * x + 1],
            device_id=(partner,),
            device_id_type=MESH,
        )

    tell = [
        pair_copy(where_hbm, pair_where, 0),
        pair_copy(owner_hbm, pair_owners, 1),
    ]

    def wanted(table, at):
        places = first_two([table[j] // RD != at for j in range(RD)])
        found = []
        for place in places:
            item = table[jnp.maximum(place, 0)]
            device = item // RD
            here = jnp.logical_and(place >= 0, device % 2 == core)
            found.append((place, device // 2, item % RD, here))
        return found

    def forward(buf, found):
        return two_rows(
            [
                jnp.where(here, pick_marked(buf[core, at], index), 0.0)
                for _, at, index, here in found
            ]
        )

    def far_rows(buf, relay, found):
        passed = relay[1].astype(F32)
        return [
            jnp.where(here, pick_marked(buf[core, at], index), passed[i : i + 1])
            for i, (_, at, index, here) in enumerate(found)
        ]

    def segment(g):
        for load in loads[3 * g : 3 * g + 3]:
            load.wait()
        start, stop = CUTS[g]

        attend(start, stop, qkv, att)

    for load in small:
        load.wait()
    own = head_mask()
    mine = first[...].astype(F32)[:8]
    far_requests = wanted(where, me)
    far_slots = wanted(owners, me)
    places = [place for place, _, _, _ in far_requests]
    no_stats = jnp.zeros((1, 2 * HD), F32)
    qg[core, chip] = message(
        [jnp.concatenate([pick_row(mine[:, :D], j), no_stats], axis=1) for j in places], places
    )
    def attend_local():
        row8 = lax.broadcasted_iota(jnp.int32, (8, EXT), 0)
        held = jnp.zeros((8, EXT), F32)
        parts = partials(
            [mine[j : j + 1, :D] for j in range(RD)],
            [where[j] % RD for j in range(RD)],
            cache,
            lengths,
            own,
        )
        for j, part in enumerate(parts):
            held = jnp.where(row8 == j, part, held)
        local_part[...] = held

    pl.semaphore_wait(barrier, nc)
    start_chips(qg, 0, [far_first(t) for t in range(nc - 1)])
    for copy in tell:
        copy.start()
    segment(0)
    segment(1)
    segment(2)
    for copy in tell:
        copy.wait_recv()
    pair_requests = wanted(pair_where, partner)
    pair_slots = wanted(pair_owners, partner)
    all_chips(qg, 0).wait_recv()
    relay_q[0] = forward(qg, pair_slots)
    pass_q = pair_copy(relay_q.at[0], relay_q.at[1], 2)
    pass_q.start()
    load_cache.wait()
    pass_q.wait_recv()

    places = [place for place, _, _, _ in far_slots]
    rows = partials(
        [q[:, :D] for q in far_rows(qg, relay_q, far_slots)],
        [jnp.maximum(place, 0) for place in places],
        cache,
        lengths,
        own,
    )
    cg[core, chip] = message(rows, places)

    to_first(cg.at[core, chip]).start()
    start_chips(cg, 1, [peer(0)])
    start_chips(cg, 1, [peer(t) for t in range(1, nc - 1)])
    attend_local()
    load_weight.wait()
    load_hidden.wait()
    is_prefill = flag[0] == 1

    own_scores = []
    for j in range(RD):
        product = mine[j : j + 1, :D] * mine[j : j + 1, D : 2 * D]
        own_scores.append(
            jnp.sum(jnp.where(own, product, 0.0), axis=1, keepdims=True) * SCALE
        )


    @pl.loop(0, D // NT)
    def _(n):
        cols = pl.ds(pl.multiple_of(n * NT, NT), NT)
        rows = pl.ds(UP, TOK_DEV - UP)
        acc = jnp.dot(att[rows, :], weight[:, cols], preferred_element_type=F32)
        acc = jnp.where(is_prefill, acc, 0.0).astype(BF16).astype(F32)
        low[:, cols] = (hidden[:, cols].astype(F32) + acc).astype(BF16)

    all_chips(cg, 1).wait_recv()
    pass_c = pair_copy(relay_c.at[0], relay_c.at[1], 3)

    @pl.when(chip > 0)
    def _():
        relay_c[0] = forward(cg, pair_requests)
        pass_c.start()
        pass_c.wait()

    @pl.when(chip == 0)
    def _():
        to_first(cg.at[1 - core]).wait_recv()
        relay_c[1] = two_rows(
            [pick_marked(cg[1 - core, at], index) for _, at, index, _ in far_requests]
        )


    row16 = lax.broadcasted_iota(jnp.int32, (H, D), 0)
    row_h = lax.broadcasted_iota(jnp.int32, (H, HD), 0)
    lane_h = lax.broadcasted_iota(jnp.int32, (H, HD), 1)
    diagonal = lane_h % H == row_h
    is_max = jnp.logical_and(diagonal, lane_h < 3 * H)
    is_total = jnp.logical_and(
        diagonal, jnp.logical_and(lane_h >= 3 * H, lane_h < 6 * H)
    )
    decoded = jnp.zeros((H, D), F32)
    places = [place for place, _, _, _ in far_requests]
    fars = far_rows(cg, relay_c, far_requests)
    for j in range(RD):
        part = jnp.where(places[0] == j, fars[0], local_part[j : j + 1, :])
        part = jnp.where(places[1] == j, fars[1], part)
        co = part[:, :D]
        cm = jnp.sum(jnp.where(is_max, part[:, D : D + HD], 0.0), axis=1, keepdims=True)
        cl = jnp.sum(jnp.where(is_total, part[:, D : D + HD], 0.0), axis=1, keepdims=True)
        row = mine[j : j + 1]
        ns = own_scores[j]
        joint = jnp.maximum(cm, ns)
        wc = jnp.exp(cm - joint)
        wo = jnp.exp(ns - joint)
        whole = cl * wc + wo
        mixed = co * (wc / whole) + row[:, 2 * D :] * (wo / whole)
        decoded = jnp.where(
            row16 == j, jnp.sum(jnp.where(own, mixed, 0.0), axis=0, keepdims=True), decoded
        )
    kept = jnp.where(is_prefill, att[pl.ds(0, H), :].astype(F32), decoded)
    att[pl.ds(0, H), :] = kept.astype(BF16)
    all_chips(qg, 0).wait_send()
    all_chips(cg, 1).wait_send()
    to_first(cg.at[core, chip]).wait_send()
    for copy in [*tell, pass_q]:
        copy.wait_send()


def finish(flag, att, low, weight, hidden, out_hbm, out, sem):
    is_prefill = flag[0] == 1
    store_low = pltpu.make_async_copy(low, out_hbm.at[pl.ds(UP, TOK_DEV - UP), :], sem.at[0])
    store_low.start()

    def project(rows, n):
        cols = pl.ds(n * COLS, COLS)
        acc = jnp.dot(att[pl.ds(0, rows), :], weight[:, cols], preferred_element_type=F32)
        acc = acc.astype(BF16).astype(F32)
        out[pl.ds(0, rows), cols] = (hidden[pl.ds(0, rows), cols].astype(F32) + acc).astype(BF16)
        store = pltpu.make_async_copy(
            out.at[pl.ds(0, rows), cols], out_hbm.at[pl.ds(0, rows), cols], sem.at[2 + n]
        )
        store.start()
        return store

    @pl.when(is_prefill)
    def _():
        for store in [project(UP, n) for n in range(D // COLS)]:
            store.wait()

    @pl.when(jnp.logical_not(is_prefill))
    def _():
        rest = pl.ds(H, UP - H)
        store_rest = pltpu.make_async_copy(hidden.at[rest, :], out_hbm.at[rest, :], sem.at[1])
        store_rest.start()
        for store in [project(H, n) for n in range(D // COLS)]:
            store.wait()
        store_rest.wait()

    store_low.wait()


def local(hidden_in, qkv, cache, lengths, prefill_flag, cache_slot, slot_owner, out_weight, n):
    nc = n // 2
    hbm = pl.BlockSpec(memory_space=pltpu.HBM)
    dma = pltpu.SemaphoreType.DMA
    vmem = pl.BlockSpec(memory_space=pltpu.VMEM)
    keep = [
        jax.ShapeDtypeStruct((TOK_DEV, D), BF16),
        jax.ShapeDtypeStruct((TOK_DEV - UP, D), BF16),
        jax.ShapeDtypeStruct((D, D), BF16),
    ]
    args = [
        x if x.shape == (1,) else pltpu.with_memory_space_constraint(x, pltpu.HBM)
        for x in (lengths, prefill_flag, cache_slot, slot_owner, hidden_in, qkv, cache, out_weight)
    ]
    kept = pl.pallas_call(
        functools.partial(kernel, nc),
        out_shape=keep,
        in_specs=[hbm, pl.BlockSpec(memory_space=pltpu.SMEM)] + [hbm] * 6,
        out_specs=[vmem] * 3,
        scratch_shapes=[
            pltpu.SMEM((RD,), jnp.int32),
            pltpu.SMEM((RD,), jnp.int32),
            pltpu.SMEM((RD,), jnp.int32),
            pltpu.SMEM((RD,), jnp.int32),
            pltpu.SMEM((RD,), jnp.int32),
            pltpu.VMEM((16, 3 * D), BF16),
            pltpu.VMEM((TOK_DEV - UP, D), BF16),
            pltpu.VMEM((3, TOK_DEV, D), BF16),
            pltpu.VMEM((RD, LMAX, 2 * D), BF16),
            pltpu.VMEM((8, EXT), F32),
            pltpu.VMEM((2, nc, 2, EXT), BF16),
            pltpu.VMEM((2, nc, 2, EXT), BF16),
            pltpu.VMEM((2, 2, EXT), BF16),
            pltpu.VMEM((2, 2, EXT), BF16),
            dma((8 + 3 * len(CUTS),)),
            dma((6,)),
            dma((8,)),
        ],
        compiler_params=pltpu.CompilerParams(
            collective_id=0, has_side_effects=True, vmem_limit_bytes=34 * 1024 * 1024
        ),
    )(*args)
    return pl.pallas_call(
        finish,
        out_shape=jax.ShapeDtypeStruct((TOK_DEV, D), BF16),
        in_specs=[pl.BlockSpec(memory_space=pltpu.SMEM)] + [vmem] * 4,
        out_specs=hbm,
        scratch_shapes=[pltpu.VMEM((UP, D), BF16), dma((2 + D // COLS,))],
        compiler_params=pltpu.CompilerParams(vmem_limit_bytes=34 * 1024 * 1024),
    )(prefill_flag, *kept, hidden_in)


def solution(mesh):
    placed = (
        P("req", None),
        P("req", None),
        P("req", None, None),
        P("req"),
        P("req"),
        P("req"),
        P("req"),
        P(),
    )
    return jax.shard_map(
        functools.partial(local, n=mesh.shape["req"]),
        mesh=mesh,
        in_specs=placed,
        out_specs=P("req", None),
        check_vma=False,
    )
```
